32 devices in a mesh: energy: 8 (over y, x, core), space: 4 (over z).
Axes of the slice: x: 2, y: 2, z: 4, core: 2. Of those that a mesh axis runs over, the one named last changes fastest.
Arguments:
- green: bfloat16 [4, 8, 4, 384, 384], P(None, 'energy', 'space'), may hold values from -6 to 6
- v_diag: bfloat16 [4, 384, 384], P('space'), may hold values from -0.3125 to 0.3125
- v_low: bfloat16 [4, 384, 384], P('space'), may hold values from -0.3125 to 0.3125
- energy_slot: int32 [8], replicated, may hold values from 0 to 7, each once
Outputs:
- sigma: bfloat16 [2, 8, 4, 384, 384], P(None, None, 'space', 'energy')
The draws below stay inside these ranges and needn't reach their ends.
Inputs may be any that keep to these rules, and one draw needn't show every extreme that they name: `energy_slot`: each grid energy appears in exactly one slot.
All inputs are finite; a program needn't handle non-finite values.
Results may differ from the reference program's by a relative error of at most 0.0066.
Values may be sent and summed in bfloat16 or wider, within the bound.
No kernel may reach another device: no remote copies, remote signals or barrier semaphores. Data moves between devices by JAX's collectives and lax.ppermute only.
A program may use at most 64 MiB of HBM per device.

```python
import jax
import jax.numpy as jnp
from jax import lax

B = 384
NE = 8
NB = 4


def level_of(own_key, shape, cuts, low, largest):
    def one(position, shards_of):
        steps = jax.random.uniform(jax.random.fold_in(jax.random.fold_in(own_key, 6), position), (shards_of,), jnp.float32, low / len(cuts), largest / len(cuts))
        return jnp.repeat(jnp.exp(steps), shape[position] // shards_of).reshape((-1,) + (1,) * (len(shape) - position - 1))

    factor_of = one(*cuts[0])
    for cut in cuts[1:]:
        factor_of = factor_of * one(*cut)
    return factor_of


def scatter_about(stream_key, shape, deviation, bound, split=(), kind=jnp.bfloat16):
    gain = level_of(stream_key, shape, split, -0.22, 0.18) if split else 1.0
    values = jax.random.normal(stream_key, shape, jnp.float32) * deviation * gain
    return jnp.minimum(jnp.maximum(values, -bound), bound).astype(kind)


def setup_inputs(seed: int = 0) -> dict:
    seeds = jax.random.split(jax.random.key(seed), 5)
    green = scatter_about(seeds[0], (4, NE, NB, B, B), 1.0, 6.0, ((1, 8), (2, 4)))
    v_diag = scatter_about(seeds[1], (NB, B, B), B ** -0.5, 0.3125, ((0, 4),))
    v_low = scatter_about(seeds[2], (NB, B, B), B ** -0.5, 0.3125, ((0, 4),))
    energy_slot = jax.random.permutation(seeds[3], NE).astype(jnp.int32)
    return {"green": green, "v_diag": v_diag, "v_low": v_low, "energy_slot": energy_slot}


def correlate_polar(grid):
    count = grid.shape[1]
    lesser = grid[0:2]
    greater = grid[2:4]
    padded = jnp.concatenate([lesser, jnp.zeros_like(lesser)], axis=1)

    def advance(offset, result):
        moved = lax.dynamic_slice_in_dim(padded, offset, count, 1)
        real_part = jnp.sum(moved[1] * greater[0] - moved[0] * greater[1], axis=0)
        imag_part = -jnp.sum(moved[0] * greater[0] + moved[1] * greater[1], axis=0)
        value = jnp.stack([real_part, imag_part])[:, None]
        return lax.dynamic_update_slice_in_dim(result, value, offset, 1)

    result = lax.fori_loop(0, count, advance, jnp.zeros_like(lesser))
    return result * (count ** -0.5)


def correlate_sigma(lesser, screened):
    count = lesser.shape[1]
    padded = jnp.concatenate([jnp.zeros_like(lesser), lesser], axis=1)

    def advance(offset, total):
        moved = lax.dynamic_slice_in_dim(padded, count - offset, count, 1)
        w_real = lax.dynamic_index_in_dim(screened[0], offset, 0, keepdims=True)
        w_imag = lax.dynamic_index_in_dim(screened[1], offset, 0, keepdims=True)
        real_part = -(moved[0] * w_imag + moved[1] * w_real)
        imag_part = moved[0] * w_real - moved[1] * w_imag
        return total + jnp.stack([real_part, imag_part])

    total = lax.fori_loop(0, count, advance, jnp.zeros_like(lesser))
    return total * (count ** -0.5)


def sandwich(matrix, polar):
    left = jnp.einsum("ij,cejk->ceik", matrix.astype(jnp.float32), polar.astype(jnp.float32)).astype(jnp.bfloat16)
    return jnp.einsum("ceij,kj->ceik", left.astype(jnp.float32), matrix.astype(jnp.float32))


def sandwich_t(matrix, polar):
    left = jnp.einsum("ji,cejk->ceik", matrix.astype(jnp.float32), polar.astype(jnp.float32)).astype(jnp.bfloat16)
    return jnp.einsum("ceij,jk->ceik", left.astype(jnp.float32), matrix.astype(jnp.float32))


def reference(green, v_diag, v_low, energy_slot):
    count = green.shape[1]
    blocks = green.shape[2]
    inverse = jnp.zeros((count,), jnp.int32).at[energy_slot].set(jnp.arange(count, dtype=jnp.int32))
    indices = jnp.arange(blocks, dtype=jnp.int32)

    def polar_block(index):
        block = green[:, :, index].astype(jnp.float32)[:, inverse]
        return correlate_polar(block).astype(jnp.bfloat16)[:, energy_slot]

    polar = lax.map(polar_block, indices)
    zero = jnp.zeros_like(polar[0])

    def sigma_block(index):
        own_polar = polar[index]
        below = jnp.where(index > 0, polar[jnp.maximum(index - 1, 0)], zero)
        above = jnp.where(index < blocks - 1, polar[jnp.minimum(index + 1, blocks - 1)], zero)
        coupling_up = v_low[jnp.minimum(index + 1, blocks - 1)]
        upper = lax.optimization_barrier(sandwich_t(coupling_up, above).astype(jnp.bfloat16)).astype(jnp.float32)
        total = sandwich(v_diag[index], own_polar) + sandwich(v_low[index], below) + upper
        screened = total.astype(jnp.bfloat16)[:, inverse].astype(jnp.float32)
        lesser = green[0:2, :, index].astype(jnp.float32)[:, inverse]
        return correlate_sigma(lesser, screened).astype(jnp.bfloat16)[:, energy_slot]

    sigma = lax.map(sigma_block, indices)
    return jnp.moveaxis(sigma, 0, 2)
```

```python
import functools
import math

import jax
import jax.numpy as jnp
from jax import lax
from jax.experimental import pallas as pl
from jax.experimental.pallas import tpu as pltpu
from jax.sharding import PartitionSpec as P


F32 = jnp.float32
BF16 = jnp.bfloat16
LANES = 128
SUBLANES = 16
PAIRED = 16
VMEM_LIMIT = 16 * 2**20


def vmem():
    return pl.BlockSpec(memory_space=pltpu.VMEM)


def smem():
    return pl.BlockSpec(memory_space=pltpu.SMEM)


def row_tile(rows):
    return 8 if rows % 8 == 0 else rows


def for_tiles(rows, cols, body):
    height = row_tile(rows)
    down = rows // height
    across = cols // LANES

    def step(index, carry):
        row = pl.multiple_of((index // across) * height, height)
        col = pl.multiple_of((index % across) * LANES, LANES)
        body((pl.ds(row, height), pl.ds(col, LANES)))
        return carry

    lax.fori_loop(0, down * across, step, 0)


def polar_kernel(order, scaling, *refs):
    count = (len(refs) - 4) // 2
    slot_ref = refs[0]
    pieces = refs[1 : 1 + count]
    outs = refs[1 + count : 1 + 2 * count]
    lesser, greater, polar = refs[1 + 2 * count :]
    energies, rows, cols = lesser.shape[1:]
    for j in range(count):
        grid = slot_ref[order(j)]
        for part in range(2):
            lesser[part, grid] = pieces[j][part].astype(F32)
            greater[part, grid] = pieces[j][part + 2].astype(F32)

    def body(tile):
        low_re = [lesser[(0, g) + tile] for g in range(energies)]
        low_im = [lesser[(1, g) + tile] for g in range(energies)]
        high_re = [greater[(0, g) + tile] for g in range(energies)]
        high_im = [greater[(1, g) + tile] for g in range(energies)]
        for w in range(energies):
            real = imag = None
            for g in range(energies - w):
                a, b, c, d = low_re[g + w], low_im[g + w], high_re[g], high_im[g]
                one = b * c - a * d
                two = a * c + b * d
                real = one if real is None else real + one
                imag = two if imag is None else imag + two
            polar[(w, 0) + tile] = real * scaling
            polar[(w, 1) + tile] = imag * -scaling

    for_tiles(rows, cols, body)
    for j in range(count):
        outs[j][...] = polar[order(j)].astype(BF16)


def sigma_kernel(order, scaling, *refs):
    count = len(refs) - 5
    slot_ref = refs[0]
    pieces = refs[1 : 1 + count]
    lesser, out, weight, total = refs[1 + count :]
    energies, rows, cols = lesser.shape[1:]
    for j in range(count):
        weight[order(j)] = pieces[j][...].astype(F32)

    def body(tile):
        low_re = [lesser[(0, g) + tile] for g in range(energies)]
        low_im = [lesser[(1, g) + tile] for g in range(energies)]
        w_re = [weight[(w, 0) + tile] for w in range(energies)]
        w_im = [weight[(w, 1) + tile] for w in range(energies)]
        for e in range(energies):
            real = imag = None
            for w in range(e + 1):
                a, b, c, d = low_re[e - w], low_im[e - w], w_re[w], w_im[w]
                one = a * d + b * c
                two = a * c - b * d
                real = one if real is None else real + one
                imag = two if imag is None else imag + two
            total[(0, e) + tile] = real * -scaling
            total[(1, e) + tile] = imag * scaling

    for_tiles(rows, cols, body)
    for s in range(energies):
        for part in range(2):
            out[part, s, 0] = total[part, slot_ref[s]].astype(BF16)


def dot(a, b, dims):
    return lax.dot_general(a, b, (dims, ((), ())), preferred_element_type=F32)


NN = ((1,), (0,))
NT = ((1,), (1,))
TN = ((0,), (0,))


def gather_kernel(order, *refs):
    pieces, out = refs[:-1], refs[-1]
    rows = pieces[0].shape[1]
    for j, piece in enumerate(pieces):
        at = pl.multiple_of(order(j) * rows, rows)
        for part in range(2):
            out[part, pl.ds(at, rows)] = piece[part]


def own_kernel(vd, polar, out):
    for part in range(2):
        left = dot(vd[...], polar[part], NN).astype(BF16)
        out[part] = dot(left, vd[...], NT)


def screen_kernel(order, vl, vu, own, below, above, *refs):
    outs, total = refs[:-1], refs[-1]
    for part in range(2):
        left = dot(vl[...], below[part], NN).astype(BF16)
        lower = dot(left, vl[...], NT)
        left = dot(vu[...], above[part], TN).astype(BF16)
        upper = dot(left, vu[...], NN).astype(BF16).astype(F32)
        total[part] = (own[part] + lower + upper).astype(BF16)
    rows = outs[0].shape[1]
    for j, out in enumerate(outs):
        at = pl.multiple_of(order(j) * rows, rows)
        for part in range(2):
            out[part] = total[part, pl.ds(at, rows)]


def call(kernel, name, outs, args, tables=0, scratch=(), flops=0):
    traffic = sum(x.size * x.dtype.itemsize for x in (*args, *outs))
    return pl.pallas_call(
        kernel,
        name=name,
        out_shape=outs,
        in_specs=[smem()] * tables + [vmem()] * (len(args) - tables),
        out_specs=[vmem()] * len(outs),
        scratch_shapes=scratch,
        compiler_params=pltpu.CompilerParams(vmem_limit_bytes=VMEM_LIMIT),
        cost_estimate=pl.CostEstimate(flops=flops, bytes_accessed=traffic, transcendentals=0),
    )(*args)


def struct(shape, kind=BF16):
    return jax.ShapeDtypeStruct(shape, kind)


def direct(energies, green, v_diag, v_low, energy_slot):
    parts = lax.axis_size("energy")
    layers = lax.axis_size("space")
    block, cols = green.shape[3:]
    rows = block // parts
    scaling = energies ** (-0.5)
    me = lax.axis_index("energy")

    def order(j):
        return lax.axis_index("energy") ^ j

    def swap(pieces):
        out = [pieces[0]]
        for j in range(1, parts):
            out.append(lax.ppermute(pieces[j], "energy", [(i, i ^ j) for i in range(parts)]))
        return out

    def shift(value, steps):
        pairs = [(i, i + steps) for i in range(layers) if 0 <= i + steps < layers]
        return lax.ppermute(value, "space", pairs)

    cut = [lax.dynamic_slice_in_dim(green[:, 0, 0], (me ^ j) * rows, rows, 1) for j in range(parts)]
    arrived = swap(cut)
    upper = shift(v_low[0], -1)
    arrived[0], upper = lax.optimization_barrier((arrived[0], upper))
    piece = struct((2, rows, cols))
    *polar_out, lesser = call(
        functools.partial(polar_kernel, order, scaling),
        "polar",
        [piece] * parts + [struct((2, energies, rows, cols), F32)],
        [energy_slot] + arrived,
        tables=1,
        scratch=[pltpu.VMEM((2, energies, rows, cols), F32), pltpu.VMEM((energies, 2, rows, cols), F32)],
    )
    polar_in = swap(polar_out)
    whole = struct((2, block, cols))
    polar = call(functools.partial(gather_kernel, order), "gather", [whole], polar_in)[0]
    below = shift(polar, 1)
    above = shift(polar, -1)
    work = 4 * block * block * cols
    own = call(own_kernel, "own", [struct(whole.shape, F32)], [v_diag[0], polar], flops=2 * work)[0]
    screened_out = call(
        functools.partial(screen_kernel, order),
        "screen",
        [piece] * parts,
        [v_low[0], upper, own, below, above],
        scratch=[pltpu.VMEM(whole.shape, BF16)],
        flops=4 * work,
    )
    screened_in = swap(screened_out)
    return call(
        functools.partial(sigma_kernel, order, scaling),
        "sigma",
        [struct((2, energies, 1, rows, cols))],
        [energy_slot] + screened_in + [lesser],
        tables=1,
        scratch=[pltpu.VMEM((energies, 2, rows, cols), F32), pltpu.VMEM((2, energies, rows, cols), F32)],
    )[0]


def shifted(value, axis, steps):
    count = lax.axis_size(axis)
    leading, last = (max(0, -steps), min(count, count - steps))
    return lax.ppermute(value, axis, [(source, source + steps) for source in range(leading, last)])


def apply_table(table, values):
    return jnp.dot(
        table, values, precision=lax.Precision.HIGHEST, preferred_element_type=jnp.float32
    )


def spectra(cos_table, sin_table, real_part, imag_part):
    out_real = apply_table(cos_table, real_part) + apply_table(sin_table, imag_part)
    out_imag = apply_table(cos_table, imag_part) - apply_table(sin_table, real_part)
    return (out_real, out_imag)


def to_slots(cos_table, sin_table, real_part, imag_part):
    factor = 1.0 / cos_table.shape[0]
    cos_back = cos_table.T
    sin_back = sin_table.T
    out_real = (apply_table(cos_back, real_part) - apply_table(sin_back, imag_part)) * factor
    out_imag = (apply_table(cos_back, imag_part) + apply_table(sin_back, real_part)) * factor
    return (out_real, out_imag)


def sandwich(matrix, polar):
    left = jnp.einsum("ij,cejk->ceik", matrix, polar, preferred_element_type=jnp.float32).astype(
        jnp.bfloat16
    )
    return jnp.einsum("ceij,kj->ceik", left, matrix, preferred_element_type=jnp.float32)


def sandwich_t(matrix, polar):
    left = jnp.einsum("ji,cejk->ceik", matrix, polar, preferred_element_type=jnp.float32).astype(
        jnp.bfloat16
    )
    return jnp.einsum("ceij,jk->ceik", left, matrix, preferred_element_type=jnp.float32)


def general(green, v_diag, v_low, energy_slot):
    energies = energy_slot.shape[0]
    period = 2 * energies
    frequency = jnp.arange(period, dtype=jnp.int32)
    phases = frequency[:, None] * energy_slot[None, :] % period
    angles = phases.astype(jnp.float32) * (2.0 * math.pi / period)
    cos_table = jnp.cos(angles)
    sin_table = jnp.sin(angles)
    scaling = energies ** (-0.5)
    arrived = lax.all_to_all(green[:, :, 0], "energy", split_axis=2, concat_axis=1, tiled=True)
    row_count = arrived.shape[2]
    col_count = arrived.shape[3]
    flattened = arrived.reshape((4, energies, row_count * col_count)).astype(jnp.float32)
    lesser_re, lesser_im = spectra(cos_table, sin_table, flattened[0], flattened[1])
    greater_re, greater_im = spectra(cos_table, sin_table, flattened[2], flattened[3])
    cross_re = lesser_re * greater_re + lesser_im * greater_im
    cross_im = lesser_im * greater_re - lesser_re * greater_im
    corr_re, corr_im = to_slots(cos_table, sin_table, cross_re, cross_im)
    polar_slot = (
        jnp.stack([corr_im * scaling, -corr_re * scaling])
        .reshape((2, energies, row_count, col_count))
        .astype(jnp.bfloat16)
    )
    polar = lax.all_to_all(polar_slot, "energy", split_axis=1, concat_axis=2, tiled=True)
    diagonal = v_diag[0]
    lower = v_low[0]
    own_term = sandwich(diagonal, polar)
    below = shifted(polar, "space", 1)
    handed = sandwich_t(lower, polar).astype(jnp.bfloat16)
    received = shifted(handed, "space", -1)
    total = own_term + sandwich(lower, below) + received.astype(jnp.float32)
    screened = total.astype(jnp.bfloat16)
    screened_rows = lax.all_to_all(screened, "energy", split_axis=2, concat_axis=1, tiled=True)
    weights = screened_rows.reshape((2, energies, row_count * col_count)).astype(jnp.float32)
    weight_re, weight_im = spectra(cos_table, sin_table, weights[0], weights[1])
    joint_re = lesser_re * weight_re - lesser_im * weight_im
    joint_im = lesser_re * weight_im + lesser_im * weight_re
    conv_re, conv_im = to_slots(cos_table, sin_table, joint_re, joint_im)
    sigma = (
        jnp.stack([-conv_im * scaling, conv_re * scaling])
        .reshape((2, energies, row_count, col_count))
        .astype(jnp.bfloat16)
    )
    return sigma[:, :, None]


def solution(mesh):
    in_specs = (
        P(None, "energy", "space", None, None),
        P("space", None, None),
        P("space", None, None),
        P(),
    )
    out_specs = P(None, None, "space", "energy", None)

    def whole(green, v_diag, v_low, energy_slot):
        parts = mesh.shape["energy"]
        rows = green.shape[3] // parts
        paired = parts & (parts - 1) == 0 and parts == energy_slot.shape[0] and parts <= PAIRED
        body = functools.partial(direct, parts) if paired and rows % SUBLANES == 0 else general
        return jax.shard_map(body, mesh=mesh, in_specs=in_specs, out_specs=out_specs, check_vma=False)(
            green, v_diag, v_low, energy_slot
        )

    return whole
```

```python
import functools
import math

import jax
import jax.numpy as jnp
from jax import lax
from jax.experimental import pallas as pl
from jax.experimental.pallas import tpu as pltpu
from jax.sharding import PartitionSpec as P


F32 = jnp.float32
BF16 = jnp.bfloat16
LANES = 128
SUBLANES = 16
PAIRED = 16
VMEM_LIMIT = 16 * 2**20


def vmem():
    return pl.BlockSpec(memory_space=pltpu.VMEM)


def smem():
    return pl.BlockSpec(memory_space=pltpu.SMEM)


def row_tile(rows):
    return 8 if rows % 8 == 0 else rows


def for_tiles(rows, cols, body):
    height = row_tile(rows)
    down = rows // height
    across = cols // LANES

    def step(index, carry):
        row = pl.multiple_of((index // across) * height, height)
        col = pl.multiple_of((index % across) * LANES, LANES)
        body((pl.ds(row, height), pl.ds(col, LANES)))
        return carry

    lax.fori_loop(0, down * across, step, 0)


def polar_kernel(order, scaling, *refs):
    count = (len(refs) - 4) // 2
    slot_ref = refs[0]
    pieces = refs[1 : 1 + count]
    outs = refs[1 + count : 1 + 2 * count]
    lesser, greater, polar = refs[1 + 2 * count :]
    energies, rows, cols = lesser.shape[1:]
    for j in range(count):
        grid = slot_ref[order(j)]
        for part in range(2):
            lesser[part, grid] = pieces[j][part].astype(F32)
            greater[part, grid] = pieces[j][part + 2].astype(F32)

    def body(tile):
        low_re = [lesser[(0, g) + tile] for g in range(energies)]
        low_im = [lesser[(1, g) + tile] for g in range(energies)]
        high_re = [greater[(0, g) + tile] for g in range(energies)]
        high_im = [greater[(1, g) + tile] for g in range(energies)]
        for w in range(energies):
            real = imag = None
            for g in range(energies - w):
                a, b, c, d = low_re[g + w], low_im[g + w], high_re[g], high_im[g]
                one = b * c - a * d
                two = a * c + b * d
                real = one if real is None else real + one
                imag = two if imag is None else imag + two
            polar[(w, 0) + tile] = real * scaling
            polar[(w, 1) + tile] = imag * -scaling

    for_tiles(rows, cols, body)
    for j in range(count):
        outs[j][...] = polar[order(j)].astype(BF16)


def sigma_kernel(order, scaling, *refs):
    count = len(refs) - 5
    slot_ref = refs[0]
    pieces = refs[1 : 1 + count]
    lesser, out, weight, total = refs[1 + count :]
    energies, rows, cols = lesser.shape[1:]
    for j in range(count):
        weight[order(j)] = pieces[j][...].astype(F32)

    def body(tile):
        low_re = [lesser[(0, g) + tile] for g in range(energies)]
        low_im = [lesser[(1, g) + tile] for g in range(energies)]
        w_re = [weight[(w, 0) + tile] for w in range(energies)]
        w_im = [weight[(w, 1) + tile] for w in range(energies)]
        for e in range(energies):
            real = imag = None
            for w in range(e + 1):
                a, b, c, d = low_re[e - w], low_im[e - w], w_re[w], w_im[w]
                one = a * d + b * c
                two = a * c - b * d
                real = one if real is None else real + one
                imag = two if imag is None else imag + two
            total[(0, e) + tile] = real * -scaling
            total[(1, e) + tile] = imag * scaling

    for_tiles(rows, cols, body)
    for s in range(energies):
        for part in range(2):
            out[part, s, 0] = total[part, slot_ref[s]].astype(BF16)


def dot(a, b, dims):
    return lax.dot_general(a, b, (dims, ((), ())), preferred_element_type=F32)


NN = ((1,), (0,))
NT = ((1,), (1,))
TN = ((0,), (0,))


def gather_kernel(order, *refs):
    pieces, out = refs[:-1], refs[-1]
    rows = pieces[0].shape[1]
    for j, piece in enumerate(pieces):
        at = pl.multiple_of((order(j) % len(pieces)) * rows, rows)
        for part in range(2):
            out[part, pl.ds(at, rows)] = piece[part]


def join(order, halves, whole):
    height = halves[0].shape[1]
    parts = whole.shape[1] // height
    mine = order(0) // (lax.axis_size("energy") // parts)
    for j, half in enumerate(halves):
        at = pl.multiple_of((mine ^ j) * height, height)
        whole[:, pl.ds(at, height)] = half[...]


def own_kernel(order, vd, *refs):
    halves, out, polar = refs[:-2], refs[-2], refs[-1]
    join(order, halves, polar)
    for part in range(2):
        left = dot(vd[...], polar[part], NN).astype(BF16)
        out[part] = dot(left, vd[...], NT)


def screen_kernel(order, count, vl, own, *refs):
    vu = refs[0:2]
    polar = refs[2 : 2 + count], refs[2 + count : 2 + 2 * count]
    outs, whole, total = refs[2 + 2 * count : -2], refs[-2], refs[-1]
    for pair in range(2):
        join(order, polar[pair], whole.at[pair])
    even = lax.axis_index("space") % 2 == 0

    def screen(upper, below, above):
        for part in range(2):
            left = dot(vl[...], below[part], NN).astype(BF16)
            lower = dot(left, vl[...], NT)
            left = dot(upper[...], above[part], TN).astype(BF16)
            raised = dot(left, upper[...], NN).astype(BF16).astype(F32)
            total[part] = (own[part] + lower + raised).astype(BF16)

    @pl.when(even)
    def _():
        screen(vu[0], whole.at[1], whole.at[0])

    @pl.when(jnp.logical_not(even))
    def _():
        screen(vu[1], whole.at[0], whole.at[1])

    rows = outs[0].shape[1]
    for j, out in enumerate(outs):
        at = pl.multiple_of(order(j) * rows, rows)
        for part in range(2):
            out[part] = total[part, pl.ds(at, rows)]


def call(kernel, outs, args, tables=0, scratch=(), flops=0):
    traffic = sum(x.size * x.dtype.itemsize for x in (*args, *outs))
    return pl.pallas_call(
        kernel,
        out_shape=outs,
        in_specs=[smem()] * tables + [vmem()] * (len(args) - tables),
        out_specs=[vmem()] * len(outs),
        scratch_shapes=scratch,
        compiler_params=pltpu.CompilerParams(vmem_limit_bytes=VMEM_LIMIT),
        cost_estimate=pl.CostEstimate(flops=flops, bytes_accessed=traffic, transcendentals=0),
    )(*args)


def struct(shape, kind=BF16):
    return jax.ShapeDtypeStruct(shape, kind)


def direct(energies, green, v_diag, v_low, energy_slot):
    parts = lax.axis_size("energy")
    layers = lax.axis_size("space")
    block, cols = green.shape[3:]
    rows = block // parts
    scaling = energies ** (-0.5)
    me = lax.axis_index("energy")

    def order(j):
        return lax.axis_index("energy") ^ j

    def swap(pieces, sequence):
        out = list(pieces)
        for j in sequence:
            out[j] = lax.ppermute(pieces[j], "energy", [(i, i ^ j) for i in range(parts)])
        return out

    def meet(value):
        out = []
        for first in range(2):
            lows = range(first, layers - 1, 2)
            out.append(lax.ppermute(value, "space", [p for i in lows for p in ((i, i + 1), (i + 1, i))]))
        return out

    cut = [lax.dynamic_slice_in_dim(green[:, 0, 0], (me ^ j) * rows, rows, 1) for j in range(parts)]
    arrived = swap(cut, range(1, parts))
    upper = meet(v_low[0])
    arrived[0], *upper = lax.optimization_barrier((arrived[0], *upper))
    piece = struct((2, rows, cols))
    *polar_out, lesser = call(
        functools.partial(polar_kernel, order, scaling),
        [piece] * parts + [struct((2, energies, rows, cols), F32)],
        [energy_slot] + arrived,
        tables=1,
        scratch=[pltpu.VMEM((2, energies, rows, cols), F32), pltpu.VMEM((energies, 2, rows, cols), F32)],
    )
    polar_in = swap(polar_out, range(1, parts))
    half = parts // 2
    part = struct((2, block // 2, cols))
    whole = struct((2, block, cols))
    own_halves, halves = [], ([], [])
    for h in range(2):
        pieces = polar_in[h * half : (h + 1) * half]
        own_halves.append(call(functools.partial(gather_kernel, order), [part], pieces)[0])
        for pair, value in enumerate(meet(own_halves[h])):
            halves[pair].append(value)
    work = 4 * block * block * cols
    own = call(
        functools.partial(own_kernel, order),
        [struct(whole.shape, F32)],
        [v_diag[0], *own_halves],
        scratch=[pltpu.VMEM(whole.shape, BF16)],
        flops=2 * work,
    )[0]
    screened_out = call(
        functools.partial(screen_kernel, order, 2),
        [piece] * parts,
        [v_low[0], own, *upper, *halves[0], *halves[1]],
        scratch=[pltpu.VMEM((2, *whole.shape), BF16), pltpu.VMEM(whole.shape, BF16)],
        flops=4 * work,
    )
    screened_in = swap(screened_out, range(1, parts))
    return call(
        functools.partial(sigma_kernel, order, scaling),
        [struct((2, energies, 1, rows, cols))],
        [energy_slot] + screened_in + [lesser],
        tables=1,
        scratch=[pltpu.VMEM((energies, 2, rows, cols), F32), pltpu.VMEM((2, energies, rows, cols), F32)],
    )[0]


def shifted(value, axis, steps):
    count = lax.axis_size(axis)
    leading, last = (max(0, -steps), min(count, count - steps))
    return lax.ppermute(value, axis, [(source, source + steps) for source in range(leading, last)])


def apply_table(table, values):
    return jnp.dot(
        table, values, precision=lax.Precision.HIGHEST, preferred_element_type=jnp.float32
    )


def spectra(cos_table, sin_table, real_part, imag_part):
    out_real = apply_table(cos_table, real_part) + apply_table(sin_table, imag_part)
    out_imag = apply_table(cos_table, imag_part) - apply_table(sin_table, real_part)
    return (out_real, out_imag)


def to_slots(cos_table, sin_table, real_part, imag_part):
    factor = 1.0 / cos_table.shape[0]
    cos_back = cos_table.T
    sin_back = sin_table.T
    out_real = (apply_table(cos_back, real_part) - apply_table(sin_back, imag_part)) * factor
    out_imag = (apply_table(cos_back, imag_part) + apply_table(sin_back, real_part)) * factor
    return (out_real, out_imag)


def sandwich(matrix, polar):
    left = jnp.einsum("ij,cejk->ceik", matrix, polar, preferred_element_type=jnp.float32).astype(
        jnp.bfloat16
    )
    return jnp.einsum("ceij,kj->ceik", left, matrix, preferred_element_type=jnp.float32)


def sandwich_t(matrix, polar):
    left = jnp.einsum("ji,cejk->ceik", matrix, polar, preferred_element_type=jnp.float32).astype(
        jnp.bfloat16
    )
    return jnp.einsum("ceij,jk->ceik", left, matrix, preferred_element_type=jnp.float32)


def general(green, v_diag, v_low, energy_slot):
    energies = energy_slot.shape[0]
    period = 2 * energies
    frequency = jnp.arange(period, dtype=jnp.int32)
    phases = frequency[:, None] * energy_slot[None, :] % period
    angles = phases.astype(jnp.float32) * (2.0 * math.pi / period)
    cos_table = jnp.cos(angles)
    sin_table = jnp.sin(angles)
    scaling = energies ** (-0.5)
    arrived = lax.all_to_all(green[:, :, 0], "energy", split_axis=2, concat_axis=1, tiled=True)
    row_count = arrived.shape[2]
    col_count = arrived.shape[3]
    flattened = arrived.reshape((4, energies, row_count * col_count)).astype(jnp.float32)
    lesser_re, lesser_im = spectra(cos_table, sin_table, flattened[0], flattened[1])
    greater_re, greater_im = spectra(cos_table, sin_table, flattened[2], flattened[3])
    cross_re = lesser_re * greater_re + lesser_im * greater_im
    cross_im = lesser_im * greater_re - lesser_re * greater_im
    corr_re, corr_im = to_slots(cos_table, sin_table, cross_re, cross_im)
    polar_slot = (
        jnp.stack([corr_im * scaling, -corr_re * scaling])
        .reshape((2, energies, row_count, col_count))
        .astype(jnp.bfloat16)
    )
    polar = lax.all_to_all(polar_slot, "energy", split_axis=1, concat_axis=2, tiled=True)
    diagonal = v_diag[0]
    lower = v_low[0]
    own_term = sandwich(diagonal, polar)
    below = shifted(polar, "space", 1)
    handed = sandwich_t(lower, polar).astype(jnp.bfloat16)
    received = shifted(handed, "space", -1)
    total = own_term + sandwich(lower, below) + received.astype(jnp.float32)
    screened = total.astype(jnp.bfloat16)
    screened_rows = lax.all_to_all(screened, "energy", split_axis=2, concat_axis=1, tiled=True)
    weights = screened_rows.reshape((2, energies, row_count * col_count)).astype(jnp.float32)
    weight_re, weight_im = spectra(cos_table, sin_table, weights[0], weights[1])
    joint_re = lesser_re * weight_re - lesser_im * weight_im
    joint_im = lesser_re * weight_im + lesser_im * weight_re
    conv_re, conv_im = to_slots(cos_table, sin_table, joint_re, joint_im)
    sigma = (
        jnp.stack([-conv_im * scaling, conv_re * scaling])
        .reshape((2, energies, row_count, col_count))
        .astype(jnp.bfloat16)
    )
    return sigma[:, :, None]


def solution(mesh):
    in_specs = (
        P(None, "energy", "space", None, None),
        P("space", None, None),
        P("space", None, None),
        P(),
    )
    out_specs = P(None, None, "space", "energy", None)
    parts = mesh.shape["energy"]
    paired = parts & (parts - 1) == 0 and 1 < parts <= PAIRED and mesh.shape["space"] > 2

    def whole(green, v_diag, v_low, energy_slot):
        rows = green.shape[3] // parts
        fast = paired and parts == energy_slot.shape[0] and rows % SUBLANES == 0
        body = functools.partial(direct, parts) if fast else general
        return jax.shard_map(body, mesh=mesh, in_specs=in_specs, out_specs=out_specs, check_vma=False)(
            green, v_diag, v_low, energy_slot
        )

    return whole
```

```python
import functools
import math

import jax
import jax.numpy as jnp
from jax import lax
from jax.experimental import pallas as pl
from jax.experimental.pallas import tpu as pltpu
from jax.sharding import PartitionSpec as P


F32 = jnp.float32
BF16 = jnp.bfloat16
LANES = 128
SUBLANES = 16
PAIRED = 16
VMEM_LIMIT = 16 * 2**20


def vmem():
    return pl.BlockSpec(memory_space=pltpu.VMEM)


def smem():
    return pl.BlockSpec(memory_space=pltpu.SMEM)


def row_tile(rows):
    return 8 if rows % 8 == 0 else rows


def for_tiles(rows, cols, body):
    height = row_tile(rows)
    down = rows // height
    across = cols // LANES

    def step(index, carry):
        row = pl.multiple_of((index // across) * height, height)
        col = pl.multiple_of((index % across) * LANES, LANES)
        body((pl.ds(row, height), pl.ds(col, LANES)))
        return carry

    lax.fori_loop(0, down * across, step, 0)


def cut_kernel(order, partners, green, *refs):
    outs, sems = refs[:-1], refs[-1]
    rows = outs[0].shape[1]
    copies = []
    for i, (j, out) in enumerate(zip(partners, outs)):
        at = pl.multiple_of(order(j) * rows, rows)
        copies.append(pltpu.make_async_copy(green.at[:, 0, 0, pl.ds(at, rows)], out, sems.at[i]))
    for copy in copies:
        copy.start()
    for copy in copies:
        copy.wait()


def polar_kernel(order, scaling, *refs):
    count = (len(refs) - 4) // 2
    slot_ref = refs[0]
    pieces = refs[1 : 1 + count]
    outs = refs[1 + count : 1 + 2 * count]
    lesser, greater, polar = refs[1 + 2 * count :]
    energies, rows, cols = lesser.shape[1:]
    for j in range(count):
        grid = slot_ref[order(j)]
        for part in range(2):
            lesser[part, grid] = pieces[j][part].astype(F32)
            greater[part, grid] = pieces[j][part + 2].astype(F32)

    def body(tile):
        low_re = [lesser[(0, g) + tile] for g in range(energies)]
        low_im = [lesser[(1, g) + tile] for g in range(energies)]
        high_re = [greater[(0, g) + tile] for g in range(energies)]
        high_im = [greater[(1, g) + tile] for g in range(energies)]
        for w in range(energies):
            real = imag = None
            for g in range(energies - w):
                a, b, c, d = low_re[g + w], low_im[g + w], high_re[g], high_im[g]
                one = b * c - a * d
                two = a * c + b * d
                real = one if real is None else real + one
                imag = two if imag is None else imag + two
            polar[(w, 0) + tile] = real * scaling
            polar[(w, 1) + tile] = imag * -scaling

    for_tiles(rows, cols, body)
    for j in range(count):
        outs[j][...] = polar[order(j)].astype(BF16)


def sigma_kernel(order, scaling, *refs):
    count = len(refs) - 5
    slot_ref = refs[0]
    pieces = refs[1 : 1 + count]
    lesser, out, weight, total = refs[1 + count :]
    energies, rows, cols = lesser.shape[1:]
    for j in range(count):
        weight[order(j)] = pieces[j][...].astype(F32)

    def body(tile):
        low_re = [lesser[(0, g) + tile] for g in range(energies)]
        low_im = [lesser[(1, g) + tile] for g in range(energies)]
        w_re = [weight[(w, 0) + tile] for w in range(energies)]
        w_im = [weight[(w, 1) + tile] for w in range(energies)]
        for e in range(energies):
            real = imag = None
            for w in range(e + 1):
                a, b, c, d = low_re[e - w], low_im[e - w], w_re[w], w_im[w]
                one = a * d + b * c
                two = a * c - b * d
                real = one if real is None else real + one
                imag = two if imag is None else imag + two
            total[(0, e) + tile] = real * -scaling
            total[(1, e) + tile] = imag * scaling

    for_tiles(rows, cols, body)
    for s in range(energies):
        for part in range(2):
            out[part, s, 0] = total[part, slot_ref[s]].astype(BF16)


def dot(a, b, dims):
    return lax.dot_general(a, b, (dims, ((), ())), preferred_element_type=F32)


NN = ((1,), (0,))
NT = ((1,), (1,))
TN = ((0,), (0,))


def gather_kernel(order, *refs):
    pieces, out = refs[:-1], refs[-1]
    rows = pieces[0].shape[1]
    for j, piece in enumerate(pieces):
        at = pl.multiple_of((order(j) % len(pieces)) * rows, rows)
        for part in range(2):
            out[part, pl.ds(at, rows)] = piece[part]


def join(order, halves, whole):
    height = halves[0].shape[1]
    parts = whole.shape[1] // height
    mine = order(0) // (lax.axis_size("energy") // parts)
    for j, half in enumerate(halves):
        at = pl.multiple_of((mine ^ j) * height, height)
        whole[:, pl.ds(at, height)] = half[...]


def own_kernel(order, vd, *refs):
    halves, out, polar = refs[:-2], refs[-2], refs[-1]
    join(order, halves, polar)
    for part in range(2):
        left = dot(vd[...], polar[part], NN).astype(BF16)
        out[part] = dot(left, vd[...], NT)


def screen_kernel(order, count, vl, own, *refs):
    vu = refs[0:2]
    polar = refs[2 : 2 + count], refs[2 + count : 2 + 2 * count]
    outs, whole, total = refs[2 + 2 * count : -2], refs[-2], refs[-1]
    for pair in range(2):
        join(order, polar[pair], whole.at[pair])
    even = lax.axis_index("space") % 2 == 0

    def screen(upper, below, above):
        for part in range(2):
            left = dot(vl[...], below[part], NN).astype(BF16)
            lower = dot(left, vl[...], NT)
            left = dot(upper[...], above[part], TN).astype(BF16)
            raised = dot(left, upper[...], NN).astype(BF16).astype(F32)
            total[part] = (own[part] + lower + raised).astype(BF16)

    @pl.when(even)
    def _():
        screen(vu[0], whole.at[1], whole.at[0])

    @pl.when(jnp.logical_not(even))
    def _():
        screen(vu[1], whole.at[0], whole.at[1])

    rows = outs[0].shape[1]
    for j, out in enumerate(outs):
        at = pl.multiple_of(order(j) * rows, rows)
        for part in range(2):
            out[part] = total[part, pl.ds(at, rows)]


def call(kernel, outs, args, tables=0, scratch=(), flops=0):
    traffic = sum(x.size * x.dtype.itemsize for x in (*args, *outs))
    return pl.pallas_call(
        kernel,
        out_shape=outs,
        in_specs=[smem()] * tables + [vmem()] * (len(args) - tables),
        out_specs=[vmem()] * len(outs),
        scratch_shapes=scratch,
        compiler_params=pltpu.CompilerParams(vmem_limit_bytes=VMEM_LIMIT),
        cost_estimate=pl.CostEstimate(flops=flops, bytes_accessed=traffic, transcendentals=0),
    )(*args)


def struct(shape, kind=BF16):
    return jax.ShapeDtypeStruct(shape, kind)


def direct(energies, green, v_diag, v_low, energy_slot):
    parts = lax.axis_size("energy")
    layers = lax.axis_size("space")
    block, cols = green.shape[3:]
    rows = block // parts
    scaling = energies ** (-0.5)

    def order(j):
        return lax.axis_index("energy") ^ j

    def swap(pieces, sequence):
        out = list(pieces)
        for j in sequence:
            out[j] = lax.ppermute(pieces[j], "energy", [(i, i ^ j) for i in range(parts)])
        return out

    def meet(value):
        out = []
        for first in range(2):
            lows = range(first, layers - 1, 2)
            out.append(lax.ppermute(value, "space", [p for i in lows for p in ((i, i + 1), (i + 1, i))]))
        return out

    def take(partners):
        return pl.pallas_call(
            functools.partial(cut_kernel, order, partners),
            out_shape=[struct((green.shape[0], rows, cols))] * len(partners),
            in_specs=[pl.BlockSpec(memory_space=pltpu.HBM)],
            out_specs=[vmem()] * len(partners),
            scratch_shapes=[pltpu.SemaphoreType.DMA((len(partners),))],
            compiler_params=pltpu.CompilerParams(vmem_limit_bytes=VMEM_LIMIT),
        )(pltpu.with_memory_space_constraint(green, pltpu.HBM))

    first, later = sequence_far(parts)[:2], (*sequence_far(parts)[2:], 0)
    cut = dict(zip(first + later, (*take(first), *take(later))))
    cut = [cut[j] for j in range(parts)]
    arrived = swap(cut, range(1, parts))
    upper = meet(v_low[0])
    piece = struct((2, rows, cols))
    *polar_out, lesser = call(
        functools.partial(polar_kernel, order, scaling),
        [piece] * parts + [struct((2, energies, rows, cols), F32)],
        [energy_slot] + arrived,
        tables=1,
        scratch=[pltpu.VMEM((2, energies, rows, cols), F32), pltpu.VMEM((energies, 2, rows, cols), F32)],
    )
    polar_in = swap(polar_out, range(1, parts))
    half = parts // 2
    part = struct((2, block // 2, cols))
    whole = struct((2, block, cols))
    own_halves, halves = [], ([], [])
    for h in range(2):
        pieces = polar_in[h * half : (h + 1) * half]
        own_halves.append(call(functools.partial(gather_kernel, order), [part], pieces)[0])
        for pair, value in enumerate(meet(own_halves[h])):
            halves[pair].append(value)
    work = 4 * block * block * cols
    own = call(
        functools.partial(own_kernel, order),
        [struct(whole.shape, F32)],
        [v_diag[0], *own_halves],
        scratch=[pltpu.VMEM(whole.shape, BF16)],
        flops=2 * work,
    )[0]
    screened_out = call(
        functools.partial(screen_kernel, order, 2),
        [piece] * parts,
        [v_low[0], own, *upper, *halves[0], *halves[1]],
        scratch=[pltpu.VMEM((2, *whole.shape), BF16), pltpu.VMEM(whole.shape, BF16)],
        flops=4 * work,
    )
    screened_in = swap(screened_out, range(1, parts))
    return call(
        functools.partial(sigma_kernel, order, scaling),
        [struct((2, energies, 1, rows, cols))],
        [energy_slot] + screened_in + [lesser],
        tables=1,
        scratch=[pltpu.VMEM((energies, 2, rows, cols), F32), pltpu.VMEM((2, energies, rows, cols), F32)],
    )[0]


def shifted(value, axis, steps):
    count = lax.axis_size(axis)
    leading, last = (max(0, -steps), min(count, count - steps))
    return lax.ppermute(value, axis, [(source, source + steps) for source in range(leading, last)])


def apply_table(table, values):
    return jnp.dot(
        table, values, precision=lax.Precision.HIGHEST, preferred_element_type=jnp.float32
    )


def spectra(cos_table, sin_table, real_part, imag_part):
    out_real = apply_table(cos_table, real_part) + apply_table(sin_table, imag_part)
    out_imag = apply_table(cos_table, imag_part) - apply_table(sin_table, real_part)
    return (out_real, out_imag)


def to_slots(cos_table, sin_table, real_part, imag_part):
    factor = 1.0 / cos_table.shape[0]
    cos_back = cos_table.T
    sin_back = sin_table.T
    out_real = (apply_table(cos_back, real_part) - apply_table(sin_back, imag_part)) * factor
    out_imag = (apply_table(cos_back, imag_part) + apply_table(sin_back, real_part)) * factor
    return (out_real, out_imag)


def sandwich(matrix, polar):
    left = jnp.einsum("ij,cejk->ceik", matrix, polar, preferred_element_type=jnp.float32).astype(
        jnp.bfloat16
    )
    return jnp.einsum("ceij,kj->ceik", left, matrix, preferred_element_type=jnp.float32)


def sandwich_t(matrix, polar):
    left = jnp.einsum("ji,cejk->ceik", matrix, polar, preferred_element_type=jnp.float32).astype(
        jnp.bfloat16
    )
    return jnp.einsum("ceij,jk->ceik", left, matrix, preferred_element_type=jnp.float32)


def general(green, v_diag, v_low, energy_slot):
    energies = energy_slot.shape[0]
    period = 2 * energies
    frequency = jnp.arange(period, dtype=jnp.int32)
    phases = frequency[:, None] * energy_slot[None, :] % period
    angles = phases.astype(jnp.float32) * (2.0 * math.pi / period)
    cos_table = jnp.cos(angles)
    sin_table = jnp.sin(angles)
    scaling = energies ** (-0.5)
    arrived = lax.all_to_all(green[:, :, 0], "energy", split_axis=2, concat_axis=1, tiled=True)
    row_count = arrived.shape[2]
    col_count = arrived.shape[3]
    flattened = arrived.reshape((4, energies, row_count * col_count)).astype(jnp.float32)
    lesser_re, lesser_im = spectra(cos_table, sin_table, flattened[0], flattened[1])
    greater_re, greater_im = spectra(cos_table, sin_table, flattened[2], flattened[3])
    cross_re = lesser_re * greater_re + lesser_im * greater_im
    cross_im = lesser_im * greater_re - lesser_re * greater_im
    corr_re, corr_im = to_slots(cos_table, sin_table, cross_re, cross_im)
    polar_slot = (
        jnp.stack([corr_im * scaling, -corr_re * scaling])
        .reshape((2, energies, row_count, col_count))
        .astype(jnp.bfloat16)
    )
    polar = lax.all_to_all(polar_slot, "energy", split_axis=1, concat_axis=2, tiled=True)
    diagonal = v_diag[0]
    lower = v_low[0]
    own_term = sandwich(diagonal, polar)
    below = shifted(polar, "space", 1)
    handed = sandwich_t(lower, polar).astype(jnp.bfloat16)
    received = shifted(handed, "space", -1)
    total = own_term + sandwich(lower, below) + received.astype(jnp.float32)
    screened = total.astype(jnp.bfloat16)
    screened_rows = lax.all_to_all(screened, "energy", split_axis=2, concat_axis=1, tiled=True)
    weights = screened_rows.reshape((2, energies, row_count * col_count)).astype(jnp.float32)
    weight_re, weight_im = spectra(cos_table, sin_table, weights[0], weights[1])
    joint_re = lesser_re * weight_re - lesser_im * weight_im
    joint_im = lesser_re * weight_im + lesser_im * weight_re
    conv_re, conv_im = to_slots(cos_table, sin_table, joint_re, joint_im)
    sigma = (
        jnp.stack([-conv_im * scaling, conv_re * scaling])
        .reshape((2, energies, row_count, col_count))
        .astype(jnp.bfloat16)
    )
    return sigma[:, :, None]


def sequence_far(parts):
    return (*(j + core for j in (6, 4, 2) if j < parts for core in range(2)), *range(8, parts), 1)


def solution(mesh):
    in_specs = (
        P(None, "energy", "space", None, None),
        P("space", None, None),
        P("space", None, None),
        P(),
    )
    out_specs = P(None, None, "space", "energy", None)
    parts = mesh.shape["energy"]
    paired = parts & (parts - 1) == 0 and 1 < parts <= PAIRED and mesh.shape["space"] > 2

    def whole(green, v_diag, v_low, energy_slot):
        rows = green.shape[3] // parts
        fast = paired and parts == energy_slot.shape[0] and rows % SUBLANES == 0
        body = functools.partial(direct, parts) if fast else general
        return jax.shard_map(body, mesh=mesh, in_specs=in_specs, out_specs=out_specs, check_vma=False)(
            green, v_diag, v_low, energy_slot
        )

    return whole
```

```python
import functools
import math

import jax
import jax.numpy as jnp
from jax import lax
from jax.experimental import pallas as pl
from jax.experimental.pallas import tpu as pltpu
from jax.sharding import PartitionSpec as P


F32 = jnp.float32
BF16 = jnp.bfloat16
LANES = 128
SUBLANES = 16
PAIRED = 16
VMEM_LIMIT = 20 * 2**20


def vmem():
    return pl.BlockSpec(memory_space=pltpu.VMEM)


def smem():
    return pl.BlockSpec(memory_space=pltpu.SMEM)


def row_tile(rows):
    return 8 if rows % 8 == 0 else rows


def for_tiles(rows, cols, body, start=0):
    height = row_tile(rows)
    down = rows // height
    across = cols // LANES

    def step(index, carry):
        row = pl.multiple_of(start + (index // across) * height, height)
        col = pl.multiple_of((index % across) * LANES, LANES)
        body((pl.ds(row, height), pl.ds(col, LANES)))
        return carry

    lax.fori_loop(0, down * across, step, 0, unroll=2)


def sum_of(terms):
    return functools.reduce(lambda x, y: x + y, terms)


def cut_kernel(order, partners, green, *refs):
    outs, sems = refs[:-1], refs[-1]
    rows = outs[0].shape[1]
    copies = []
    for i, (j, out) in enumerate(zip(partners, outs)):
        at = pl.multiple_of(order(j) * rows, rows)
        copies.append(pltpu.make_async_copy(green.at[:, 0, 0, pl.ds(at, rows)], out, sems.at[i]))
    for copy in copies:
        copy.start()
    for copy in copies:
        copy.wait()


def polar_kernel(order, scaling, *refs):
    count = (len(refs) - 4) // 2
    slot_ref = refs[0]
    pieces = refs[1 : 1 + count]
    outs = refs[1 + count : 1 + 2 * count]
    lesser, greater, polar = refs[1 + 2 * count :]
    energies, rows, cols = lesser.shape[1:]
    for j in range(count):
        grid = slot_ref[order(j)]
        for part in range(2):
            lesser[part, grid] = pieces[j][part].astype(F32)
            greater[part, grid] = pieces[j][part + 2].astype(F32)

    def body(tile):
        low_re = [lesser[(0, g) + tile] for g in range(energies)]
        low_im = [lesser[(1, g) + tile] for g in range(energies)]
        high_re = [greater[(0, g) + tile] for g in range(energies)]
        high_im = [greater[(1, g) + tile] for g in range(energies)]
        low_sum = [a + b for a, b in zip(low_re, low_im)]
        high_sum = [c + d for c, d in zip(high_re, high_im)]
        high_gap = [c - d for c, d in zip(high_re, high_im)]
        for w in range(energies):
            shifted = range(energies - w)
            one = sum_of(high_re[g] * low_sum[g + w] for g in shifted)
            two = sum_of(low_re[g + w] * high_sum[g] for g in shifted)
            three = sum_of(low_im[g + w] * high_gap[g] for g in shifted)
            polar[(w, 0) + tile] = (one - two) * scaling
            polar[(w, 1) + tile] = (one - three) * -scaling

    for_tiles(rows, cols, body)
    for j in range(count):
        outs[j][...] = polar[order(j)].astype(BF16)


def sigma_kernel(order, scaling, *refs):
    count = len(refs) - 7
    slot_ref = refs[0]
    pieces = refs[1 : 1 + count]
    lesser, out, weight, total, stage, sems = refs[1 + count :]
    energies, rows, cols = lesser.shape[1:]
    for j in range(count):
        weight[order(j)] = pieces[j][...].astype(F32)

    def body(tile):
        low_re = [lesser[(0, g) + tile] for g in range(energies)]
        low_im = [lesser[(1, g) + tile] for g in range(energies)]
        w_re = [weight[(w, 0) + tile] for w in range(energies)]
        w_im = [weight[(w, 1) + tile] for w in range(energies)]
        low_sum = [a + b for a, b in zip(low_re, low_im)]
        w_sum = [c + d for c, d in zip(w_re, w_im)]
        w_gap = [d - c for c, d in zip(w_re, w_im)]
        for e in range(energies):
            one = sum_of(w_re[w] * low_sum[e - w] for w in range(e + 1))
            two = sum_of(low_re[e - w] * w_gap[w] for w in range(e + 1))
            three = sum_of(low_im[e - w] * w_sum[w] for w in range(e + 1))
            total[(0, e) + tile] = (one + two) * -scaling
            total[(1, e) + tile] = (one - three) * scaling

    copies = []
    height = SUBLANES
    for chunk in range(rows // height):
        at = pl.ds(chunk * height, height)
        for_tiles(height, cols, body, chunk * height)
        for s in range(energies):
            for part in range(2):
                stage[part, s, at] = total[part, slot_ref[s], at].astype(BF16)
        copies.append(pltpu.make_async_copy(stage.at[:, :, at], out.at[:, :, 0, at], sems.at[chunk]))
        copies[-1].start()
    for copy in copies:
        copy.wait()


def dot(a, b, dims):
    return lax.dot_general(a, b, (dims, ((), ())), preferred_element_type=F32)


NN = ((1,), (0,))
NT = ((1,), (1,))


def gather_kernel(order, *refs):
    pieces, out = refs[:-1], refs[-1]
    rows = pieces[0].shape[1]
    for j, piece in enumerate(pieces):
        at = pl.multiple_of((order(j) % len(pieces)) * rows, rows)
        for part in range(2):
            out[part, pl.ds(at, rows)] = piece[part]


def join(order, halves, whole):
    height = halves[0].shape[1]
    parts = whole.shape[1] // height
    mine = order(0) // (lax.axis_size("energy") // parts)
    for j, half in enumerate(halves):
        at = pl.multiple_of((mine ^ j) * height, height)
        whole[:, pl.ds(at, height)] = half[...]


def own_kernel(order, vd, *refs):
    halves, out, polar = refs[:-2], refs[-2], refs[-1]
    join(order, halves, polar)
    for part in range(2):
        left = dot(vd[...], polar[part], NN).astype(BF16)
        out[part] = dot(left, vd[...], NT)


def couple_kernel(order, vl, up_even, up_odd, right, left_near, left_far):
    size = vl.shape[0]
    height = size // 2
    even = lax.axis_index("space") % 2 == 0

    def fill(first, second):
        right[pl.ds(0, size)] = first
        right[pl.ds(size, size)] = second

    @pl.when(even)
    def _():
        fill(up_even[...], vl[...].T)

    @pl.when(jnp.logical_not(even))
    def _():
        fill(vl[...].T, up_odd[...])

    mine = order(0) // (lax.axis_size("energy") // 2)
    for pair in range(2):
        for j, left in enumerate((left_near, left_far)):
            at = pl.multiple_of(pair * size + (mine ^ j) * height, height)
            left[pair] = right[pl.ds(at, height)].T


def abreast(parts, wide):
    cols = parts.shape[2]
    for part in range(2):
        wide[:, part * cols : (part + 1) * cols] = parts[part]


def near_kernel(left, even, odd, out, wide):
    for pair, met in enumerate((even, odd)):
        abreast(met, wide)
        out[pair] = dot(left[pair], wide[...], NN)


def screen_kernel(order, right, left, begun, own, even, odd, *refs):
    outs, wide, product, total = refs[:-3], *refs[-3:]
    size, cols = total.shape[1:]
    for pair, met in enumerate((even, odd)):
        abreast(met, wide)
        both = (begun[pair] + dot(left[pair], wide[...], NN)).astype(BF16)
        for part in range(2):
            product[part * size : (part + 1) * size, pair * size : (pair + 1) * size] = both[:, part * cols : (part + 1) * cols]
    for part in range(2):
        total[part] = (own[part] + dot(product[part * size : (part + 1) * size], right[...], NN)).astype(BF16)
    rows = outs[0].shape[1]
    for j, out in enumerate(outs):
        at = pl.multiple_of(order(j) * rows, rows)
        for part in range(2):
            out[part] = total[part, pl.ds(at, rows)]


def call(kernel, outs, args, tables=0, scratch=(), flops=0):
    traffic = sum(x.size * x.dtype.itemsize for x in (*args, *outs))
    return pl.pallas_call(
        kernel,
        out_shape=outs,
        in_specs=[smem()] * tables + [vmem()] * (len(args) - tables),
        out_specs=[vmem()] * len(outs),
        scratch_shapes=scratch,
        compiler_params=pltpu.CompilerParams(vmem_limit_bytes=VMEM_LIMIT),
        cost_estimate=pl.CostEstimate(flops=flops, bytes_accessed=traffic, transcendentals=0),
    )(*args)


def struct(shape, kind=BF16):
    return jax.ShapeDtypeStruct(shape, kind)


def direct(energies, green, v_diag, v_low, energy_slot):
    parts = lax.axis_size("energy")
    layers = lax.axis_size("space")
    block, cols = green.shape[3:]
    rows = block // parts
    scaling = energies ** (-0.5)

    def order(j):
        return lax.axis_index("energy") ^ j

    def swap(pieces, sequence):
        out = list(pieces)
        for j in sequence:
            out[j] = lax.ppermute(pieces[j], "energy", [(i, i ^ j) for i in range(parts)])
        return out

    def meet(value):
        out = []
        for first in range(2):
            lows = range(first, layers - 1, 2)
            out.append(lax.ppermute(value, "space", [p for i in lows for p in ((i, i + 1), (i + 1, i))]))
        return out

    def take(partners):
        return pl.pallas_call(
            functools.partial(cut_kernel, order, partners),
            out_shape=[struct((green.shape[0], rows, cols))] * len(partners),
            in_specs=[pl.BlockSpec(memory_space=pltpu.HBM)],
            out_specs=[vmem()] * len(partners),
            scratch_shapes=[pltpu.SemaphoreType.DMA((len(partners),))],
            compiler_params=pltpu.CompilerParams(vmem_limit_bytes=VMEM_LIMIT),
        )(pltpu.with_memory_space_constraint(green, pltpu.HBM))

    first, later = sequence_far(parts)[:2], (*sequence_far(parts)[2:], 0)
    cut = dict(zip(first + later, (*take(first), *take(later))))
    cut = [cut[j] for j in range(parts)]
    arrived = swap(cut, range(1, parts))
    upper = meet(v_low[0])
    piece = struct((2, rows, cols))
    *polar_out, lesser = call(
        functools.partial(polar_kernel, order, scaling),
        [piece] * parts + [struct((2, energies, rows, cols), F32)],
        [energy_slot] + arrived,
        tables=1,
        scratch=[pltpu.VMEM((2, energies, rows, cols), F32), pltpu.VMEM((energies, 2, rows, cols), F32)],
    )
    polar_in = swap(polar_out, range(1, parts))
    half = parts // 2
    part = struct((2, block // 2, cols))
    whole = struct((2, block, cols))
    own_halves, halves = [], ([], [])
    for h in range(2):
        pieces = polar_in[h * half : (h + 1) * half]
        own_halves.append(call(functools.partial(gather_kernel, order), [part], pieces)[0])
        for pair, value in enumerate(meet(own_halves[h])):
            halves[pair].append(value)
    work = 4 * block * block * cols
    own = call(
        functools.partial(own_kernel, order),
        [struct(whole.shape, F32)],
        [v_diag[0], *own_halves],
        scratch=[pltpu.VMEM(whole.shape, BF16)],
        flops=2 * work,
    )[0]
    left = struct((2, block, block // 2))
    right, left_near, left_far = call(
        functools.partial(couple_kernel, order),
        [struct((2 * block, block)), left, left],
        [v_low[0], *upper],
    )
    wide = pltpu.VMEM((block // 2, 2 * cols), BF16)
    begun = call(
        near_kernel,
        [struct((2, block, 2 * cols), F32)],
        [left_near, halves[0][0], halves[1][0]],
        scratch=[wide],
        flops=work,
    )[0]
    screened_out = call(
        functools.partial(screen_kernel, order),
        [piece] * parts,
        [right, left_far, begun, own, halves[0][1], halves[1][1]],
        scratch=[wide, pltpu.VMEM((2 * block, 2 * block), BF16), pltpu.VMEM(whole.shape, BF16)],
        flops=3 * work,
    )
    screened_in = swap(screened_out, range(1, parts))
    return pl.pallas_call(
        functools.partial(sigma_kernel, order, scaling),
        name="sigma",
        out_shape=struct((2, energies, 1, rows, cols)),
        in_specs=[smem()] + [vmem()] * (parts + 1),
        out_specs=pl.BlockSpec(memory_space=pltpu.HBM),
        scratch_shapes=[
            pltpu.VMEM((energies, 2, rows, cols), F32),
            pltpu.VMEM((2, energies, rows, cols), F32),
            pltpu.VMEM((2, energies, rows, cols), BF16),
            pltpu.SemaphoreType.DMA((rows // SUBLANES,)),
        ],
        compiler_params=pltpu.CompilerParams(vmem_limit_bytes=VMEM_LIMIT),
    )(energy_slot, *screened_in, lesser)


def shifted(value, axis, steps):
    count = lax.axis_size(axis)
    leading, last = (max(0, -steps), min(count, count - steps))
    return lax.ppermute(value, axis, [(source, source + steps) for source in range(leading, last)])


def apply_table(table, values):
    return jnp.dot(
        table, values, precision=lax.Precision.HIGHEST, preferred_element_type=jnp.float32
    )


def spectra(cos_table, sin_table, real_part, imag_part):
    out_real = apply_table(cos_table, real_part) + apply_table(sin_table, imag_part)
    out_imag = apply_table(cos_table, imag_part) - apply_table(sin_table, real_part)
    return (out_real, out_imag)


def to_slots(cos_table, sin_table, real_part, imag_part):
    factor = 1.0 / cos_table.shape[0]
    cos_back = cos_table.T
    sin_back = sin_table.T
    out_real = (apply_table(cos_back, real_part) - apply_table(sin_back, imag_part)) * factor
    out_imag = (apply_table(cos_back, imag_part) + apply_table(sin_back, real_part)) * factor
    return (out_real, out_imag)


def sandwich(matrix, polar):
    left = jnp.einsum("ij,cejk->ceik", matrix, polar, preferred_element_type=jnp.float32).astype(
        jnp.bfloat16
    )
    return jnp.einsum("ceij,kj->ceik", left, matrix, preferred_element_type=jnp.float32)


def sandwich_t(matrix, polar):
    left = jnp.einsum("ji,cejk->ceik", matrix, polar, preferred_element_type=jnp.float32).astype(
        jnp.bfloat16
    )
    return jnp.einsum("ceij,jk->ceik", left, matrix, preferred_element_type=jnp.float32)


def general(green, v_diag, v_low, energy_slot):
    energies = energy_slot.shape[0]
    period = 2 * energies
    frequency = jnp.arange(period, dtype=jnp.int32)
    phases = frequency[:, None] * energy_slot[None, :] % period
    angles = phases.astype(jnp.float32) * (2.0 * math.pi / period)
    cos_table = jnp.cos(angles)
    sin_table = jnp.sin(angles)
    scaling = energies ** (-0.5)
    arrived = lax.all_to_all(green[:, :, 0], "energy", split_axis=2, concat_axis=1, tiled=True)
    row_count = arrived.shape[2]
    col_count = arrived.shape[3]
    flattened = arrived.reshape((4, energies, row_count * col_count)).astype(jnp.float32)
    lesser_re, lesser_im = spectra(cos_table, sin_table, flattened[0], flattened[1])
    greater_re, greater_im = spectra(cos_table, sin_table, flattened[2], flattened[3])
    cross_re = lesser_re * greater_re + lesser_im * greater_im
    cross_im = lesser_im * greater_re - lesser_re * greater_im
    corr_re, corr_im = to_slots(cos_table, sin_table, cross_re, cross_im)
    polar_slot = (
        jnp.stack([corr_im * scaling, -corr_re * scaling])
        .reshape((2, energies, row_count, col_count))
        .astype(jnp.bfloat16)
    )
    polar = lax.all_to_all(polar_slot, "energy", split_axis=1, concat_axis=2, tiled=True)
    diagonal = v_diag[0]
    lower = v_low[0]
    own_term = sandwich(diagonal, polar)
    below = shifted(polar, "space", 1)
    handed = sandwich_t(lower, polar).astype(jnp.bfloat16)
    received = shifted(handed, "space", -1)
    total = own_term + sandwich(lower, below) + received.astype(jnp.float32)
    screened = total.astype(jnp.bfloat16)
    screened_rows = lax.all_to_all(screened, "energy", split_axis=2, concat_axis=1, tiled=True)
    weights = screened_rows.reshape((2, energies, row_count * col_count)).astype(jnp.float32)
    weight_re, weight_im = spectra(cos_table, sin_table, weights[0], weights[1])
    joint_re = lesser_re * weight_re - lesser_im * weight_im
    joint_im = lesser_re * weight_im + lesser_im * weight_re
    conv_re, conv_im = to_slots(cos_table, sin_table, joint_re, joint_im)
    sigma = (
        jnp.stack([-conv_im * scaling, conv_re * scaling])
        .reshape((2, energies, row_count, col_count))
        .astype(jnp.bfloat16)
    )
    return sigma[:, :, None]


def sequence_far(parts):
    return (*(j + core for j in (6, 4, 2) if j < parts for core in range(2)), *range(8, parts), 1)


def solution(mesh):
    in_specs = (
        P(None, "energy", "space", None, None),
        P("space", None, None),
        P("space", None, None),
        P(),
    )
    out_specs = P(None, None, "space", "energy", None)
    parts = mesh.shape["energy"]
    paired = parts & (parts - 1) == 0 and 1 < parts <= PAIRED and mesh.shape["space"] > 2

    def whole(green, v_diag, v_low, energy_slot):
        rows = green.shape[3] // parts
        fast = paired and parts == energy_slot.shape[0] and rows % SUBLANES == 0
        body = functools.partial(direct, parts) if fast else general
        return jax.shard_map(body, mesh=mesh, in_specs=in_specs, out_specs=out_specs, check_vma=False)(
            green, v_diag, v_low, energy_slot
        )

    return whole
```

```python
import functools
import math

import jax
import jax.numpy as jnp
from jax import lax
from jax.experimental import pallas as pl
from jax.experimental.pallas import tpu as pltpu
from jax.sharding import PartitionSpec as P


F32 = jnp.float32
BF16 = jnp.bfloat16
LANES = 128
SUBLANES = 16
PAIRED = 16
VMEM_LIMIT = 20 * 2**20


def vmem():
    return pl.BlockSpec(memory_space=pltpu.VMEM)


def smem():
    return pl.BlockSpec(memory_space=pltpu.SMEM)


def row_tile(rows):
    return 8 if rows % 8 == 0 else rows


def for_tiles(rows, cols, body, start=0):
    height = row_tile(rows)
    down = rows // height
    across = cols // LANES

    def step(index, carry):
        row = pl.multiple_of(start + (index // across) * height, height)
        col = pl.multiple_of((index % across) * LANES, LANES)
        body((pl.ds(row, height), pl.ds(col, LANES)))
        return carry

    lax.fori_loop(0, down * across, step, 0, unroll=2)


def sum_of(terms):
    return functools.reduce(lambda x, y: x + y, terms)


def frequency(device, parts):
    core, chip = device % 2, device // 2
    parity = chip
    for bit in range(1, parts.bit_length()):
        parity = parity ^ (chip >> bit)
    return 2 * chip + ((parity + core) & 1)


def on_core(core, run):
    for value in range(2):
        pl.when(core == value)(functools.partial(run, value))


def cut_kernel(order, partners, green, *refs):
    outs, sems = refs[:-1], refs[-1]
    rows = outs[0].shape[1]
    copies = []
    for i, (j, out) in enumerate(zip(partners, outs)):
        at = pl.multiple_of(order(j) * rows, rows)
        copies.append(pltpu.make_async_copy(green.at[:, 0, 0, pl.ds(at, rows)], out, sems.at[i]))
    for copy in copies:
        copy.start()
    for copy in copies:
        copy.wait()


def polar_kernel(order, scaling, *refs):
    count = (len(refs) - 4) // 2
    slot_ref = refs[0]
    pieces = refs[1 : 1 + count]
    outs = refs[1 + count : 1 + 2 * count]
    lesser, greater, polar = refs[1 + 2 * count :]
    energies, rows, cols = lesser.shape[1:]
    for j in range(count):
        grid = slot_ref[order(j)]
        for part in range(2):
            lesser[part, grid] = pieces[j][part].astype(F32)
            greater[part, grid] = pieces[j][part + 2].astype(F32)

    def body(tile):
        low_re = [lesser[(0, g) + tile] for g in range(energies)]
        low_im = [lesser[(1, g) + tile] for g in range(energies)]
        high_re = [greater[(0, g) + tile] for g in range(energies)]
        high_im = [greater[(1, g) + tile] for g in range(energies)]
        low_sum = [a + b for a, b in zip(low_re, low_im)]
        high_sum = [c + d for c, d in zip(high_re, high_im)]
        high_gap = [c - d for c, d in zip(high_re, high_im)]
        for w in range(energies):
            shifted = range(energies - w)
            one = sum_of(high_re[g] * low_sum[g + w] for g in shifted)
            two = sum_of(low_re[g + w] * high_sum[g] for g in shifted)
            three = sum_of(low_im[g + w] * high_gap[g] for g in shifted)
            polar[(w, 0) + tile] = (one - two) * scaling
            polar[(w, 1) + tile] = (one - three) * -scaling

    for_tiles(rows, cols, body)
    for j in range(count):
        outs[j][...] = polar[frequency(order(j), energies)].astype(BF16)


def lag_sums(lesser, weight, tile, energies, held):
    low_re = [lesser[(0, g) + tile] for g in range(energies)]
    low_im = [lesser[(1, g) + tile] for g in range(energies)]
    w_re = [weight[(i, 0) + tile] for i in range(len(held))]
    w_im = [weight[(i, 1) + tile] for i in range(len(held))]
    low_sum = [a + b for a, b in zip(low_re, low_im)]
    w_sum = [c + d for c, d in zip(w_re, w_im)]
    w_gap = [d - c for c, d in zip(w_re, w_im)]
    for e in range(energies):
        pairs = [(i, e - w) for i, w in enumerate(held) if w <= e]
        if not pairs:
            yield e, None, None
            continue
        one = sum_of(w_re[i] * low_sum[g] for i, g in pairs)
        two = sum_of(low_re[g] * w_gap[i] for i, g in pairs)
        three = sum_of(low_im[g] * w_sum[i] for i, g in pairs)
        yield e, one - three, one + two


def held_by(core, parts):
    return [frequency(2 * chip + core, parts) for chip in range(parts // 2)]


def early_kernel(order, lesser, *refs):
    pieces, (part, weight) = refs[:-2], refs[-2:]
    energies, rows, cols = lesser.shape[1:]
    for i, piece in enumerate(pieces):
        weight[order(2 * i) // 2] = piece[...].astype(F32)

    def run(core):
        def body(tile):
            for e, real, imag in lag_sums(lesser, weight, tile, energies, held_by(core, energies)):
                part[(0, e) + tile] = jnp.zeros_like(lesser[(0, e) + tile]) if real is None else real
                part[(1, e) + tile] = jnp.zeros_like(lesser[(0, e) + tile]) if imag is None else imag

        for_tiles(rows, cols, body)

    on_core(order(0) % 2, run)


def sigma_kernel(order, scaling, slot_ref, lesser, part, *refs):
    pieces, (out, weight, total, stage, sems) = refs[:-5], refs[-5:]
    energies, rows, cols = lesser.shape[1:]
    for i, piece in enumerate(pieces):
        weight[order(2 * i + 1) // 2] = piece[...].astype(F32)
    chunks = [pl.ds(start, SUBLANES) for start in range(0, rows, SUBLANES)]
    copies = [
        pltpu.make_async_copy(stage.at[:, :, at], out.at[:, :, 0, at], sems.at[i]) for i, at in enumerate(chunks)
    ]

    def run(core):
        def body(tile):
            for e, real, imag in lag_sums(lesser, weight, tile, energies, held_by(1 - core, energies)):
                begun_re, begun_im = part[(0, e) + tile], part[(1, e) + tile]
                total[(0, e) + tile] = (begun_im if imag is None else begun_im + imag) * -scaling
                total[(1, e) + tile] = (begun_re if real is None else begun_re + real) * scaling

        for copy, at in zip(copies, chunks):
            for_tiles(at.size, cols, body, at.start)
            for s in range(energies):
                for c in range(2):
                    stage[c, s, at] = total[c, slot_ref[s], at].astype(BF16)
            copy.start()

    on_core(order(0) % 2, run)
    for copy in copies:
        copy.wait()


def dot(a, b, dims):
    return lax.dot_general(a, b, (dims, ((), ())), preferred_element_type=F32)


NN = ((1,), (0,))
NT = ((1,), (1,))


def gather_kernel(order, *refs):
    pieces, out = refs[:-1], refs[-1]
    rows = pieces[0].shape[1]
    for j, piece in enumerate(pieces):
        at = pl.multiple_of((order(j) % len(pieces)) * rows, rows)
        for part in range(2):
            out[part, pl.ds(at, rows)] = piece[part]


def join(order, halves, whole):
    height = halves[0].shape[1]
    parts = whole.shape[1] // height
    mine = order(0) // (lax.axis_size("energy") // parts)
    for j, half in enumerate(halves):
        at = pl.multiple_of((mine ^ j) * height, height)
        whole[:, pl.ds(at, height)] = half[...]


def own_kernel(order, vd, *refs):
    halves, out, polar = refs[:-2], refs[-2], refs[-1]
    join(order, halves, polar)
    for part in range(2):
        left = dot(vd[...], polar[part], NN).astype(BF16)
        out[part] = dot(left, vd[...], NT)


def couple_kernel(order, vl, up_even, up_odd, right, left_near, left_far):
    size = vl.shape[0]
    height = size // 2
    even = lax.axis_index("space") % 2 == 0

    def fill(first, second):
        right[pl.ds(0, size)] = first
        right[pl.ds(size, size)] = second

    @pl.when(even)
    def _():
        fill(up_even[...], vl[...].T)

    @pl.when(jnp.logical_not(even))
    def _():
        fill(vl[...].T, up_odd[...])

    mine = order(0) // (lax.axis_size("energy") // 2)
    for pair in range(2):
        for j, left in enumerate((left_near, left_far)):
            at = pl.multiple_of(pair * size + (mine ^ j) * height, height)
            left[pair] = right[pl.ds(at, height)].T


def abreast(parts, wide):
    cols = parts.shape[2]
    for part in range(2):
        wide[:, part * cols : (part + 1) * cols] = parts[part]


def near_kernel(left, even, odd, out, wide):
    for pair, met in enumerate((even, odd)):
        abreast(met, wide)
        out[pair] = dot(left[pair], wide[...], NN)


def screen_kernel(order, right, left, begun, own, even, odd, *refs):
    outs, wide, product, total = refs[:-3], *refs[-3:]
    size, cols = total.shape[1:]
    for pair, met in enumerate((even, odd)):
        abreast(met, wide)
        both = (begun[pair] + dot(left[pair], wide[...], NN)).astype(BF16)
        for part in range(2):
            product[part * size : (part + 1) * size, pair * size : (pair + 1) * size] = both[:, part * cols : (part + 1) * cols]
    for part in range(2):
        total[part] = (own[part] + dot(product[part * size : (part + 1) * size], right[...], NN)).astype(BF16)
    rows = outs[0].shape[1]
    for j, out in enumerate(outs):
        at = pl.multiple_of(order(j) * rows, rows)
        for part in range(2):
            out[part] = total[part, pl.ds(at, rows)]


def call(kernel, outs, args, tables=0, scratch=(), flops=0):
    traffic = sum(x.size * x.dtype.itemsize for x in (*args, *outs))
    return pl.pallas_call(
        kernel,
        out_shape=outs,
        in_specs=[smem()] * tables + [vmem()] * (len(args) - tables),
        out_specs=[vmem()] * len(outs),
        scratch_shapes=scratch,
        compiler_params=pltpu.CompilerParams(vmem_limit_bytes=VMEM_LIMIT),
        cost_estimate=pl.CostEstimate(flops=flops, bytes_accessed=traffic, transcendentals=0),
    )(*args)


def struct(shape, kind=BF16):
    return jax.ShapeDtypeStruct(shape, kind)


def direct(energies, green, v_diag, v_low, energy_slot):
    parts = lax.axis_size("energy")
    layers = lax.axis_size("space")
    block, cols = green.shape[3:]
    rows = block // parts
    scaling = energies ** (-0.5)

    def order(j):
        return lax.axis_index("energy") ^ j

    def swap(pieces, sequence):
        out = list(pieces)
        for j in sequence:
            out[j] = lax.ppermute(pieces[j], "energy", [(i, i ^ j) for i in range(parts)])
        return out

    def meet(value):
        out = []
        for first in range(2):
            lows = range(first, layers - 1, 2)
            out.append(lax.ppermute(value, "space", [p for i in lows for p in ((i, i + 1), (i + 1, i))]))
        return out

    def take(partners):
        return pl.pallas_call(
            functools.partial(cut_kernel, order, partners),
            out_shape=[struct((green.shape[0], rows, cols))] * len(partners),
            in_specs=[pl.BlockSpec(memory_space=pltpu.HBM)],
            out_specs=[vmem()] * len(partners),
            scratch_shapes=[pltpu.SemaphoreType.DMA((len(partners),))],
            compiler_params=pltpu.CompilerParams(vmem_limit_bytes=VMEM_LIMIT),
        )(pltpu.with_memory_space_constraint(green, pltpu.HBM))

    first, later = sequence_far(parts)[:2], (*sequence_far(parts)[2:], 0)
    cut = dict(zip(first + later, (*take(first), *take(later))))
    cut = [cut[j] for j in range(parts)]
    arrived = swap(cut, range(1, parts))
    upper = meet(v_low[0])
    piece = struct((2, rows, cols))
    *polar_out, lesser = call(
        functools.partial(polar_kernel, order, scaling),
        [piece] * parts + [struct((2, energies, rows, cols), F32)],
        [energy_slot] + arrived,
        tables=1,
        scratch=[pltpu.VMEM((2, energies, rows, cols), F32), pltpu.VMEM((energies, 2, rows, cols), F32)],
    )
    polar_in = swap(polar_out, range(1, parts))
    half = parts // 2
    part = struct((2, block // 2, cols))
    whole = struct((2, block, cols))
    own_halves, halves = [], ([], [])
    for h in range(2):
        pieces = polar_in[h * half : (h + 1) * half]
        own_halves.append(call(functools.partial(gather_kernel, order), [part], pieces)[0])
        for pair, value in enumerate(meet(own_halves[h])):
            halves[pair].append(value)
    work = 4 * block * block * cols
    own = call(
        functools.partial(own_kernel, order),
        [struct(whole.shape, F32)],
        [v_diag[0], *own_halves],
        scratch=[pltpu.VMEM(whole.shape, BF16)],
        flops=2 * work,
    )[0]
    left = struct((2, block, block // 2))
    right, left_near, left_far = call(
        functools.partial(couple_kernel, order), [struct((2 * block, block)), left, left], [v_low[0], *upper]
    )
    wide = pltpu.VMEM((block // 2, 2 * cols), BF16)
    begun = call(
        near_kernel,
        [struct((2, block, 2 * cols), F32)],
        [left_near, halves[0][0], halves[1][0]],
        scratch=[wide],
        flops=work,
    )[0]
    screened_out = call(
        functools.partial(screen_kernel, order),
        [piece] * parts,
        [right, left_far, begun, own, halves[0][1], halves[1][1]],
        scratch=[wide, pltpu.VMEM((2 * block, 2 * block), BF16), pltpu.VMEM(whole.shape, BF16)],
        flops=3 * work,
    )
    screened_in = swap(screened_out, range(1, parts))
    weights = pltpu.VMEM((half, 2, rows, cols), F32)
    part = call(
        functools.partial(early_kernel, order),
        [struct((2, energies, rows, cols), F32)],
        [lesser, *screened_in[::2]],
        scratch=[weights],
    )[0]
    return pl.pallas_call(
        functools.partial(sigma_kernel, order, scaling),
        name="sigma",
        out_shape=struct((2, energies, 1, rows, cols)),
        in_specs=[smem()] + [vmem()] * (half + 2),
        out_specs=pl.BlockSpec(memory_space=pltpu.HBM),
        scratch_shapes=[
            weights,
            pltpu.VMEM((2, energies, rows, cols), F32),
            pltpu.VMEM((2, energies, rows, cols), BF16),
            pltpu.SemaphoreType.DMA((rows // SUBLANES,)),
        ],
        compiler_params=pltpu.CompilerParams(vmem_limit_bytes=VMEM_LIMIT),
    )(energy_slot, lesser, part, *screened_in[1::2])


def shifted(value, axis, steps):
    count = lax.axis_size(axis)
    leading, last = (max(0, -steps), min(count, count - steps))
    return lax.ppermute(value, axis, [(source, source + steps) for source in range(leading, last)])


def apply_table(table, values):
    return jnp.dot(
        table, values, precision=lax.Precision.HIGHEST, preferred_element_type=jnp.float32
    )


def spectra(cos_table, sin_table, real_part, imag_part):
    out_real = apply_table(cos_table, real_part) + apply_table(sin_table, imag_part)
    out_imag = apply_table(cos_table, imag_part) - apply_table(sin_table, real_part)
    return (out_real, out_imag)


def to_slots(cos_table, sin_table, real_part, imag_part):
    factor = 1.0 / cos_table.shape[0]
    cos_back = cos_table.T
    sin_back = sin_table.T
    out_real = (apply_table(cos_back, real_part) - apply_table(sin_back, imag_part)) * factor
    out_imag = (apply_table(cos_back, imag_part) + apply_table(sin_back, real_part)) * factor
    return (out_real, out_imag)


def sandwich(matrix, polar):
    left = jnp.einsum("ij,cejk->ceik", matrix, polar, preferred_element_type=jnp.float32).astype(
        jnp.bfloat16
    )
    return jnp.einsum("ceij,kj->ceik", left, matrix, preferred_element_type=jnp.float32)


def sandwich_t(matrix, polar):
    left = jnp.einsum("ji,cejk->ceik", matrix, polar, preferred_element_type=jnp.float32).astype(
        jnp.bfloat16
    )
    return jnp.einsum("ceij,jk->ceik", left, matrix, preferred_element_type=jnp.float32)


def general(green, v_diag, v_low, energy_slot):
    energies = energy_slot.shape[0]
    period = 2 * energies
    frequency = jnp.arange(period, dtype=jnp.int32)
    phases = frequency[:, None] * energy_slot[None, :] % period
    angles = phases.astype(jnp.float32) * (2.0 * math.pi / period)
    cos_table = jnp.cos(angles)
    sin_table = jnp.sin(angles)
    scaling = energies ** (-0.5)
    arrived = lax.all_to_all(green[:, :, 0], "energy", split_axis=2, concat_axis=1, tiled=True)
    row_count = arrived.shape[2]
    col_count = arrived.shape[3]
    flattened = arrived.reshape((4, energies, row_count * col_count)).astype(jnp.float32)
    lesser_re, lesser_im = spectra(cos_table, sin_table, flattened[0], flattened[1])
    greater_re, greater_im = spectra(cos_table, sin_table, flattened[2], flattened[3])
    cross_re = lesser_re * greater_re + lesser_im * greater_im
    cross_im = lesser_im * greater_re - lesser_re * greater_im
    corr_re, corr_im = to_slots(cos_table, sin_table, cross_re, cross_im)
    polar_slot = (
        jnp.stack([corr_im * scaling, -corr_re * scaling])
        .reshape((2, energies, row_count, col_count))
        .astype(jnp.bfloat16)
    )
    polar = lax.all_to_all(polar_slot, "energy", split_axis=1, concat_axis=2, tiled=True)
    diagonal = v_diag[0]
    lower = v_low[0]
    own_term = sandwich(diagonal, polar)
    below = shifted(polar, "space", 1)
    handed = sandwich_t(lower, polar).astype(jnp.bfloat16)
    received = shifted(handed, "space", -1)
    total = own_term + sandwich(lower, below) + received.astype(jnp.float32)
    screened = total.astype(jnp.bfloat16)
    screened_rows = lax.all_to_all(screened, "energy", split_axis=2, concat_axis=1, tiled=True)
    weights = screened_rows.reshape((2, energies, row_count * col_count)).astype(jnp.float32)
    weight_re, weight_im = spectra(cos_table, sin_table, weights[0], weights[1])
    joint_re = lesser_re * weight_re - lesser_im * weight_im
    joint_im = lesser_re * weight_im + lesser_im * weight_re
    conv_re, conv_im = to_slots(cos_table, sin_table, joint_re, joint_im)
    sigma = (
        jnp.stack([-conv_im * scaling, conv_re * scaling])
        .reshape((2, energies, row_count, col_count))
        .astype(jnp.bfloat16)
    )
    return sigma[:, :, None]


def sequence_far(parts):
    return (*(j + core for j in (6, 4, 2) if j < parts for core in range(2)), *range(8, parts), 1)


def solution(mesh):
    in_specs = (
        P(None, "energy", "space", None, None),
        P("space", None, None),
        P("space", None, None),
        P(),
    )
    out_specs = P(None, None, "space", "energy", None)
    parts = mesh.shape["energy"]
    paired = parts & (parts - 1) == 0 and 4 <= parts <= PAIRED and mesh.shape["space"] > 2

    def whole(green, v_diag, v_low, energy_slot):
        rows = green.shape[3] // parts
        fast = paired and parts == energy_slot.shape[0] and rows % SUBLANES == 0
        body = functools.partial(direct, parts) if fast else general
        return jax.shard_map(body, mesh=mesh, in_specs=in_specs, out_specs=out_specs, check_vma=False)(
            green, v_diag, v_low, energy_slot
        )

    return whole
```

```python
import functools
import math

import jax
import jax.numpy as jnp
from jax import lax
from jax.experimental import pallas as pl
from jax.experimental.pallas import tpu as pltpu
from jax.sharding import PartitionSpec as P


F32 = jnp.float32
BF16 = jnp.bfloat16
LANES = 128
SUBLANES = 16
TILE = 8
PAIRED = 16
VMEM_LIMIT = 20 * 2**20


def vmem():
    return pl.BlockSpec(memory_space=pltpu.VMEM)


def smem():
    return pl.BlockSpec(memory_space=pltpu.SMEM)


def row_tile(rows):
    return TILE if rows % TILE == 0 else rows


def for_tiles(rows, cols, body, start=0):
    height = row_tile(rows)
    down = rows // height
    across = cols // LANES

    def step(index, carry):
        row = pl.multiple_of(start + (index // across) * height, height)
        col = pl.multiple_of((index % across) * LANES, LANES)
        body((pl.ds(row, height), pl.ds(col, LANES)))
        return carry

    lax.fori_loop(0, down * across, step, 0, unroll=across if down == 1 else 2)


def sum_of(terms):
    return functools.reduce(lambda x, y: x + y, terms)


def frequency(device, parts):
    core, chip = device % 2, device // 2
    parity = chip
    for bit in range(1, parts.bit_length()):
        parity = parity ^ (chip >> bit)
    return 2 * chip + ((parity + core) & 1)


def on_core(core, run):
    for value in range(2):
        pl.when(core == value)(functools.partial(run, value))


def cut_kernel(order, partners, green, *refs):
    outs, sems = refs[:-1], refs[-1]
    rows = outs[0].shape[1]
    copies = []
    for i, (j, out) in enumerate(zip(partners, outs)):
        at = pl.multiple_of(order(j) * rows, rows)
        copies.append(pltpu.make_async_copy(green.at[:, 0, 0, pl.ds(at, rows)], out, sems.at[i]))
    for copy in copies:
        copy.start()
    for copy in copies:
        copy.wait()


def polar_kernel(order, scaling, *refs):
    count = (len(refs) - 4) // 2
    slot_ref = refs[0]
    pieces = refs[1 : 1 + count]
    outs = refs[1 + count : 1 + 2 * count]
    lesser, greater, polar = refs[1 + 2 * count :]
    energies, rows, cols = lesser.shape[1:]
    for j in range(count):
        grid = slot_ref[order(j)]
        for part in range(2):
            lesser[part, grid] = pieces[j][part].astype(F32)
            greater[part, grid] = pieces[j][part + 2].astype(F32)

    def body(tile):
        low_re = [lesser[(0, g) + tile] for g in range(energies)]
        low_im = [lesser[(1, g) + tile] for g in range(energies)]
        high_re = [greater[(0, g) + tile] for g in range(energies)]
        high_im = [greater[(1, g) + tile] for g in range(energies)]
        low_sum = [a + b for a, b in zip(low_re, low_im)]
        high_sum = [c + d for c, d in zip(high_re, high_im)]
        high_gap = [c - d for c, d in zip(high_re, high_im)]
        for w in range(energies):
            shifted = range(energies - w)
            one = sum_of(high_re[g] * low_sum[g + w] for g in shifted)
            two = sum_of(low_re[g + w] * high_sum[g] for g in shifted)
            three = sum_of(low_im[g + w] * high_gap[g] for g in shifted)
            polar[(w, 0) + tile] = (one - two) * scaling
            polar[(w, 1) + tile] = (one - three) * -scaling

    for_tiles(rows, cols, body)
    for j in range(count):
        outs[j][...] = polar[frequency(order(j), energies)].astype(BF16)


def lag_sums(lesser, weight, tile, energies, held):
    low_re = [lesser[(0, g) + tile] for g in range(energies)]
    low_im = [lesser[(1, g) + tile] for g in range(energies)]
    w_re = [weight[(i, 0) + tile] for i in range(len(held))]
    w_im = [weight[(i, 1) + tile] for i in range(len(held))]
    low_sum = [a + b for a, b in zip(low_re, low_im)]
    w_sum = [c + d for c, d in zip(w_re, w_im)]
    w_gap = [d - c for c, d in zip(w_re, w_im)]
    for e in range(energies):
        pairs = [(i, e - w) for i, w in enumerate(held) if w <= e]
        if not pairs:
            yield e, None, None
            continue
        one = sum_of(w_re[i] * low_sum[g] for i, g in pairs)
        two = sum_of(low_re[g] * w_gap[i] for i, g in pairs)
        three = sum_of(low_im[g] * w_sum[i] for i, g in pairs)
        yield e, one - three, one + two


def held_by(core, parts):
    return [frequency(2 * chip + core, parts) for chip in range(parts // 2)]


def early_kernel(order, lesser, *refs):
    pieces, (part, weight) = refs[:-2], refs[-2:]
    energies, rows, cols = lesser.shape[1:]
    for i, piece in enumerate(pieces):
        weight[order(2 * i) // 2] = piece[...].astype(F32)

    def run(core):
        def body(tile):
            for e, real, imag in lag_sums(lesser, weight, tile, energies, held_by(core, energies)):
                part[(0, e) + tile] = jnp.zeros_like(lesser[(0, e) + tile]) if real is None else real
                part[(1, e) + tile] = jnp.zeros_like(lesser[(0, e) + tile]) if imag is None else imag

        for_tiles(rows, cols, body)

    on_core(order(0) % 2, run)


def sigma_kernel(order, scaling, slot_ref, lesser, part, *refs):
    pieces, (out, weight, total, stage, sems) = refs[:-5], refs[-5:]
    energies, rows, cols = lesser.shape[1:]
    for i, piece in enumerate(pieces):
        weight[order(2 * i + 1) // 2] = piece[...].astype(F32)
    chunks = [pl.ds(start, TILE) for start in range(0, rows, TILE)]
    copies = [
        pltpu.make_async_copy(stage.at[:, :, at], out.at[:, :, 0, at], sems.at[i]) for i, at in enumerate(chunks)
    ]

    def run(core):
        def body(tile):
            for e, real, imag in lag_sums(lesser, weight, tile, energies, held_by(1 - core, energies)):
                begun_re, begun_im = part[(0, e) + tile], part[(1, e) + tile]
                total[(0, e) + tile] = (begun_im if imag is None else begun_im + imag) * -scaling
                total[(1, e) + tile] = (begun_re if real is None else begun_re + real) * scaling

        for copy, at in zip(copies, chunks):
            for_tiles(at.size, cols, body, at.start)
            for s in range(energies):
                for c in range(2):
                    stage[c, s, at] = total[c, slot_ref[s], at].astype(BF16)
            copy.start()

    on_core(order(0) % 2, run)
    for copy in copies:
        copy.wait()


def dot(a, b, dims):
    return lax.dot_general(a, b, (dims, ((), ())), preferred_element_type=F32)


NN = ((1,), (0,))
NT = ((1,), (1,))


def gather_kernel(order, *refs):
    pieces, out = refs[:-1], refs[-1]
    rows = pieces[0].shape[1]
    for j, piece in enumerate(pieces):
        at = pl.multiple_of((order(j) % len(pieces)) * rows, rows)
        for part in range(2):
            out[part, pl.ds(at, rows)] = piece[part]


def join(order, halves, whole):
    height = halves[0].shape[1]
    parts = whole.shape[1] // height
    mine = order(0) // (lax.axis_size("energy") // parts)
    for j, half in enumerate(halves):
        at = pl.multiple_of((mine ^ j) * height, height)
        whole[:, pl.ds(at, height)] = half[...]


def own_kernel(order, vd, *refs):
    halves, out, polar = refs[:-2], refs[-2], refs[-1]
    join(order, halves, polar)
    for part in range(2):
        left = dot(vd[...], polar[part], NN).astype(BF16)
        out[part] = dot(left, vd[...], NT)


def couple_kernel(order, vl, up_even, up_odd, right, left_near, left_far):
    size = vl.shape[0]
    height = size // 2
    even = lax.axis_index("space") % 2 == 0

    def fill(first, second):
        right[pl.ds(0, size)] = first
        right[pl.ds(size, size)] = second

    @pl.when(even)
    def _():
        fill(up_even[...], vl[...].T)

    @pl.when(jnp.logical_not(even))
    def _():
        fill(vl[...].T, up_odd[...])

    mine = order(0) // (lax.axis_size("energy") // 2)
    for pair in range(2):
        for j, left in enumerate((left_near, left_far)):
            at = pl.multiple_of(pair * size + (mine ^ j) * height, height)
            left[pair] = right[pl.ds(at, height)].T


def abreast(parts, wide):
    cols = parts.shape[2]
    for part in range(2):
        wide[:, part * cols : (part + 1) * cols] = parts[part]


def near_kernel(left, even, odd, out, wide):
    for pair, met in enumerate((even, odd)):
        abreast(met, wide)
        out[pair] = dot(left[pair], wide[...], NN)


def screen_kernel(order, right, left, begun, own, even, odd, *refs):
    outs, wide, product, total = refs[:-3], *refs[-3:]
    size, cols = total.shape[1:]
    for pair, met in enumerate((even, odd)):
        abreast(met, wide)
        both = (begun[pair] + dot(left[pair], wide[...], NN)).astype(BF16)
        for part in range(2):
            product[part * size : (part + 1) * size, pair * size : (pair + 1) * size] = both[:, part * cols : (part + 1) * cols]
    for part in range(2):
        total[part] = (own[part] + dot(product[part * size : (part + 1) * size], right[...], NN)).astype(BF16)
    rows = outs[0].shape[1]
    for j, out in enumerate(outs):
        at = pl.multiple_of(order(j) * rows, rows)
        for part in range(2):
            out[part] = total[part, pl.ds(at, rows)]


def call(kernel, outs, args, tables=0, scratch=(), flops=0):
    traffic = sum(x.size * x.dtype.itemsize for x in (*args, *outs))
    return pl.pallas_call(
        kernel,
        out_shape=outs,
        in_specs=[smem()] * tables + [vmem()] * (len(args) - tables),
        out_specs=[vmem()] * len(outs),
        scratch_shapes=scratch,
        compiler_params=pltpu.CompilerParams(vmem_limit_bytes=VMEM_LIMIT),
        cost_estimate=pl.CostEstimate(flops=flops, bytes_accessed=traffic, transcendentals=0),
    )(*args)


def struct(shape, kind=BF16):
    return jax.ShapeDtypeStruct(shape, kind)


def direct(energies, green, v_diag, v_low, energy_slot):
    parts = lax.axis_size("energy")
    layers = lax.axis_size("space")
    block, cols = green.shape[3:]
    rows = block // parts
    scaling = energies ** (-0.5)

    def order(j):
        return lax.axis_index("energy") ^ j

    def swap(pieces, sequence):
        out = list(pieces)
        for j in sequence:
            out[j] = lax.ppermute(pieces[j], "energy", [(i, i ^ j) for i in range(parts)])
        return out

    def meet(value):
        out = []
        for first in range(2):
            lows = range(first, layers - 1, 2)
            out.append(lax.ppermute(value, "space", [p for i in lows for p in ((i, i + 1), (i + 1, i))]))
        return out

    def take(partners):
        return pl.pallas_call(
            functools.partial(cut_kernel, order, partners),
            out_shape=[struct((green.shape[0], rows, cols))] * len(partners),
            in_specs=[pl.BlockSpec(memory_space=pltpu.HBM)],
            out_specs=[vmem()] * len(partners),
            scratch_shapes=[pltpu.SemaphoreType.DMA((len(partners),))],
            compiler_params=pltpu.CompilerParams(vmem_limit_bytes=VMEM_LIMIT),
        )(pltpu.with_memory_space_constraint(green, pltpu.HBM))

    first, later = sequence_far(parts)[:2], (*sequence_far(parts)[2:], 0)
    cut = dict(zip(first + later, (*take(first), *take(later))))
    cut = [cut[j] for j in range(parts)]
    arrived = swap(cut, range(1, parts))
    upper = meet(v_low[0])
    piece = struct((2, rows, cols))
    *polar_out, lesser = call(
        functools.partial(polar_kernel, order, scaling),
        [piece] * parts + [struct((2, energies, rows, cols), F32)],
        [energy_slot] + arrived,
        tables=1,
        scratch=[pltpu.VMEM((2, energies, rows, cols), F32), pltpu.VMEM((energies, 2, rows, cols), F32)],
    )
    polar_in = swap(polar_out, range(1, parts))
    half = parts // 2
    part = struct((2, block // 2, cols))
    whole = struct((2, block, cols))
    own_halves, halves = [], ([], [])
    for h in range(2):
        pieces = polar_in[h * half : (h + 1) * half]
        own_halves.append(call(functools.partial(gather_kernel, order), [part], pieces)[0])
        for pair, value in enumerate(meet(own_halves[h])):
            halves[pair].append(value)
    work = 4 * block * block * cols
    own = call(
        functools.partial(own_kernel, order),
        [struct(whole.shape, F32)],
        [v_diag[0], *own_halves],
        scratch=[pltpu.VMEM(whole.shape, BF16)],
        flops=2 * work,
    )[0]
    left = struct((2, block, block // 2))
    right, left_near, left_far = call(
        functools.partial(couple_kernel, order), [struct((2 * block, block)), left, left], [v_low[0], *upper]
    )
    wide = pltpu.VMEM((block // 2, 2 * cols), BF16)
    begun = call(
        near_kernel,
        [struct((2, block, 2 * cols), F32)],
        [left_near, halves[0][0], halves[1][0]],
        scratch=[wide],
        flops=work,
    )[0]
    screened_out = call(
        functools.partial(screen_kernel, order),
        [piece] * parts,
        [right, left_far, begun, own, halves[0][1], halves[1][1]],
        scratch=[wide, pltpu.VMEM((2 * block, 2 * block), BF16), pltpu.VMEM(whole.shape, BF16)],
        flops=3 * work,
    )
    screened_in = swap(screened_out, range(1, parts))
    weights = pltpu.VMEM((half, 2, rows, cols), F32)
    part = call(
        functools.partial(early_kernel, order),
        [struct((2, energies, rows, cols), F32)],
        [lesser, *screened_in[::2]],
        scratch=[weights],
    )[0]
    return pl.pallas_call(
        functools.partial(sigma_kernel, order, scaling),
        name="sigma",
        out_shape=struct((2, energies, 1, rows, cols)),
        in_specs=[smem()] + [vmem()] * (half + 2),
        out_specs=pl.BlockSpec(memory_space=pltpu.HBM),
        scratch_shapes=[
            weights,
            pltpu.VMEM((2, energies, rows, cols), F32),
            pltpu.VMEM((2, energies, rows, cols), BF16),
            pltpu.SemaphoreType.DMA((rows // TILE,)),
        ],
        compiler_params=pltpu.CompilerParams(vmem_limit_bytes=VMEM_LIMIT),
    )(energy_slot, lesser, part, *screened_in[1::2])


def shifted(value, axis, steps):
    count = lax.axis_size(axis)
    leading, last = (max(0, -steps), min(count, count - steps))
    return lax.ppermute(value, axis, [(source, source + steps) for source in range(leading, last)])


def apply_table(table, values):
    return jnp.dot(
        table, values, precision=lax.Precision.HIGHEST, preferred_element_type=jnp.float32
    )


def spectra(cos_table, sin_table, real_part, imag_part):
    out_real = apply_table(cos_table, real_part) + apply_table(sin_table, imag_part)
    out_imag = apply_table(cos_table, imag_part) - apply_table(sin_table, real_part)
    return (out_real, out_imag)


def to_slots(cos_table, sin_table, real_part, imag_part):
    factor = 1.0 / cos_table.shape[0]
    cos_back = cos_table.T
    sin_back = sin_table.T
    out_real = (apply_table(cos_back, real_part) - apply_table(sin_back, imag_part)) * factor
    out_imag = (apply_table(cos_back, imag_part) + apply_table(sin_back, real_part)) * factor
    return (out_real, out_imag)


def sandwich(matrix, polar):
    left = jnp.einsum("ij,cejk->ceik", matrix, polar, preferred_element_type=jnp.float32).astype(
        jnp.bfloat16
    )
    return jnp.einsum("ceij,kj->ceik", left, matrix, preferred_element_type=jnp.float32)


def sandwich_t(matrix, polar):
    left = jnp.einsum("ji,cejk->ceik", matrix, polar, preferred_element_type=jnp.float32).astype(
        jnp.bfloat16
    )
    return jnp.einsum("ceij,jk->ceik", left, matrix, preferred_element_type=jnp.float32)


def general(green, v_diag, v_low, energy_slot):
    energies = energy_slot.shape[0]
    period = 2 * energies
    frequency = jnp.arange(period, dtype=jnp.int32)
    phases = frequency[:, None] * energy_slot[None, :] % period
    angles = phases.astype(jnp.float32) * (2.0 * math.pi / period)
    cos_table = jnp.cos(angles)
    sin_table = jnp.sin(angles)
    scaling = energies ** (-0.5)
    arrived = lax.all_to_all(green[:, :, 0], "energy", split_axis=2, concat_axis=1, tiled=True)
    row_count = arrived.shape[2]
    col_count = arrived.shape[3]
    flattened = arrived.reshape((4, energies, row_count * col_count)).astype(jnp.float32)
    lesser_re, lesser_im = spectra(cos_table, sin_table, flattened[0], flattened[1])
    greater_re, greater_im = spectra(cos_table, sin_table, flattened[2], flattened[3])
    cross_re = lesser_re * greater_re + lesser_im * greater_im
    cross_im = lesser_im * greater_re - lesser_re * greater_im
    corr_re, corr_im = to_slots(cos_table, sin_table, cross_re, cross_im)
    polar_slot = (
        jnp.stack([corr_im * scaling, -corr_re * scaling])
        .reshape((2, energies, row_count, col_count))
        .astype(jnp.bfloat16)
    )
    polar = lax.all_to_all(polar_slot, "energy", split_axis=1, concat_axis=2, tiled=True)
    diagonal = v_diag[0]
    lower = v_low[0]
    own_term = sandwich(diagonal, polar)
    below = shifted(polar, "space", 1)
    handed = sandwich_t(lower, polar).astype(jnp.bfloat16)
    received = shifted(handed, "space", -1)
    total = own_term + sandwich(lower, below) + received.astype(jnp.float32)
    screened = total.astype(jnp.bfloat16)
    screened_rows = lax.all_to_all(screened, "energy", split_axis=2, concat_axis=1, tiled=True)
    weights = screened_rows.reshape((2, energies, row_count * col_count)).astype(jnp.float32)
    weight_re, weight_im = spectra(cos_table, sin_table, weights[0], weights[1])
    joint_re = lesser_re * weight_re - lesser_im * weight_im
    joint_im = lesser_re * weight_im + lesser_im * weight_re
    conv_re, conv_im = to_slots(cos_table, sin_table, joint_re, joint_im)
    sigma = (
        jnp.stack([-conv_im * scaling, conv_re * scaling])
        .reshape((2, energies, row_count, col_count))
        .astype(jnp.bfloat16)
    )
    return sigma[:, :, None]


def sequence_far(parts):
    return (*(j + core for j in (6, 4, 2) if j < parts for core in range(2)), *range(8, parts), 1)


def solution(mesh):
    in_specs = (
        P(None, "energy", "space", None, None),
        P("space", None, None),
        P("space", None, None),
        P(),
    )
    out_specs = P(None, None, "space", "energy", None)
    parts = mesh.shape["energy"]
    paired = parts & (parts - 1) == 0 and 4 <= parts <= PAIRED and mesh.shape["space"] > 2

    def whole(green, v_diag, v_low, energy_slot):
        rows = green.shape[3] // parts
        fast = paired and parts == energy_slot.shape[0] and rows % SUBLANES == 0
        body = functools.partial(direct, parts) if fast else general
        return jax.shard_map(body, mesh=mesh, in_specs=in_specs, out_specs=out_specs, check_vma=False)(
            green, v_diag, v_low, energy_slot
        )

    return whole
```

```python
import functools
import math

import jax
import jax.numpy as jnp
from jax import lax
from jax.experimental import pallas as pl
from jax.experimental.pallas import tpu as pltpu
from jax.sharding import PartitionSpec as P


F32 = jnp.float32
BF16 = jnp.bfloat16
LANES = 128
SUBLANES = 16
TILE = 8
PAIRED = 16
VMEM_LIMIT = 20 * 2**20


def vmem():
    return pl.BlockSpec(memory_space=pltpu.VMEM)


def smem():
    return pl.BlockSpec(memory_space=pltpu.SMEM)


def row_tile(rows):
    return TILE if rows % TILE == 0 else rows


def for_tiles(rows, cols, body, start=0):
    height = row_tile(rows)
    down = rows // height
    across = cols // LANES

    def step(index, carry):
        row = pl.multiple_of(start + (index // across) * height, height)
        col = pl.multiple_of((index % across) * LANES, LANES)
        body((pl.ds(row, height), pl.ds(col, LANES)))
        return carry

    lax.fori_loop(0, down * across, step, 0, unroll=across)


def sum_of(terms):
    return functools.reduce(lambda x, y: x + y, terms)


def frequency(device, parts):
    core, chip = device % 2, device // 2
    parity = chip
    for bit in range(1, parts.bit_length()):
        parity = parity ^ (chip >> bit)
    return 2 * chip + ((parity + core) & 1)


def on_core(core, run):
    for value in range(2):
        pl.when(core == value)(functools.partial(run, value))


def cut_kernel(order, partners, green, *refs):
    outs, sems = refs[:-1], refs[-1]
    rows = outs[0].shape[1]
    copies = []
    for i, (j, out) in enumerate(zip(partners, outs)):
        at = pl.multiple_of(order(j) * rows, rows)
        copies.append(pltpu.make_async_copy(green.at[:, 0, 0, pl.ds(at, rows)], out, sems.at[i]))
    for copy in copies:
        copy.start()
    for copy in copies:
        copy.wait()


def polar_kernel(order, scaling, *refs):
    count = (len(refs) - 4) // 2
    slot_ref = refs[0]
    pieces = refs[1 : 1 + count]
    outs = refs[1 + count : 1 + 2 * count]
    lesser, greater, polar = refs[1 + 2 * count :]
    energies, rows, cols = lesser.shape[1:]
    for j in range(count):
        grid = slot_ref[order(j)]
        for part in range(2):
            lesser[part, grid] = pieces[j][part].astype(F32)
            greater[part, grid] = pieces[j][part + 2].astype(F32)

    def body(tile):
        low_re = [lesser[(0, g) + tile] for g in range(energies)]
        low_im = [lesser[(1, g) + tile] for g in range(energies)]
        high_re = [greater[(0, g) + tile] for g in range(energies)]
        high_im = [greater[(1, g) + tile] for g in range(energies)]
        low_sum = [a + b for a, b in zip(low_re, low_im)]
        high_sum = [c + d for c, d in zip(high_re, high_im)]
        high_gap = [c - d for c, d in zip(high_re, high_im)]
        for w in range(energies):
            shifted = range(energies - w)
            one = sum_of(high_re[g] * low_sum[g + w] for g in shifted)
            two = sum_of(low_re[g + w] * high_sum[g] for g in shifted)
            three = sum_of(low_im[g + w] * high_gap[g] for g in shifted)
            polar[(w, 0) + tile] = (one - two) * scaling
            polar[(w, 1) + tile] = (one - three) * -scaling

    for_tiles(rows, cols, body)
    for j in range(count):
        outs[j][...] = polar[frequency(order(j), energies)].astype(BF16)


def lag_sums(lesser, weight, tile, energies, held):
    low_re = [lesser[(0, g) + tile] for g in range(energies)]
    low_im = [lesser[(1, g) + tile] for g in range(energies)]
    w_re = [weight[(i, 0) + tile] for i in range(len(held))]
    w_im = [weight[(i, 1) + tile] for i in range(len(held))]
    low_sum = [a + b for a, b in zip(low_re, low_im)]
    w_sum = [c + d for c, d in zip(w_re, w_im)]
    w_gap = [d - c for c, d in zip(w_re, w_im)]
    for e in range(energies):
        pairs = [(i, e - w) for i, w in enumerate(held) if w <= e]
        if not pairs:
            yield e, None, None
            continue
        one = sum_of(w_re[i] * low_sum[g] for i, g in pairs)
        two = sum_of(low_re[g] * w_gap[i] for i, g in pairs)
        three = sum_of(low_im[g] * w_sum[i] for i, g in pairs)
        yield e, one - three, one + two


def held_by(core, parts):
    return [frequency(2 * chip + core, parts) for chip in range(parts // 2)]


def early_kernel(order, lesser, *refs):
    pieces, (part, weight) = refs[:-2], refs[-2:]
    energies, rows, cols = lesser.shape[1:]
    for i, piece in enumerate(pieces):
        weight[order(2 * i) // 2] = piece[...].astype(F32)

    def run(core):
        def body(tile):
            for e, real, imag in lag_sums(lesser, weight, tile, energies, held_by(core, energies)):
                part[(0, e) + tile] = jnp.zeros_like(lesser[(0, e) + tile]) if real is None else real
                part[(1, e) + tile] = jnp.zeros_like(lesser[(0, e) + tile]) if imag is None else imag

        for_tiles(rows, cols, body)

    on_core(order(0) % 2, run)


def sigma_kernel(order, scaling, slot_ref, lesser, part, *refs):
    pieces, (out, weight, total, stage, sems) = refs[:-5], refs[-5:]
    energies, rows, cols = lesser.shape[1:]
    for i, piece in enumerate(pieces):
        weight[order(2 * i + 1) // 2] = piece[...].astype(F32)
    chunks = [pl.ds(start, TILE) for start in range(0, rows, TILE)]
    copies = [
        pltpu.make_async_copy(stage.at[:, :, at], out.at[:, :, 0, at], sems.at[i]) for i, at in enumerate(chunks)
    ]

    def run(core):
        def body(tile):
            for e, real, imag in lag_sums(lesser, weight, tile, energies, held_by(1 - core, energies)):
                begun_re, begun_im = part[(0, e) + tile], part[(1, e) + tile]
                total[(0, e) + tile] = (begun_im if imag is None else begun_im + imag) * -scaling
                total[(1, e) + tile] = (begun_re if real is None else begun_re + real) * scaling

        for copy, at in zip(copies, chunks):
            for_tiles(at.size, cols, body, at.start)
            for s in range(energies):
                for c in range(2):
                    stage[c, s, at] = total[c, slot_ref[s], at].astype(BF16)
            copy.start()

    on_core(order(0) % 2, run)
    for copy in copies:
        copy.wait()


def dot(a, b, dims):
    return lax.dot_general(a, b, (dims, ((), ())), preferred_element_type=F32)


NN = ((1,), (0,))
NT = ((1,), (1,))


def gather_kernel(order, *refs):
    pieces, out = refs[:-1], refs[-1]
    rows = pieces[0].shape[1]
    for j, piece in enumerate(pieces):
        at = pl.multiple_of((order(j) % len(pieces)) * rows, rows)
        for part in range(2):
            out[part, pl.ds(at, rows)] = piece[part]


def join(order, halves, whole):
    height = halves[0].shape[1]
    parts = whole.shape[1] // height
    mine = order(0) // (lax.axis_size("energy") // parts)
    for j, half in enumerate(halves):
        at = pl.multiple_of((mine ^ j) * height, height)
        whole[:, pl.ds(at, height)] = half[...]


def own_kernel(order, vd, *refs):
    halves, out, polar = refs[:-2], refs[-2], refs[-1]
    join(order, halves, polar)
    for part in range(2):
        left = dot(vd[...], polar[part], NN).astype(BF16)
        out[part] = dot(left, vd[...], NT)


def couple_kernel(order, vl, up_even, up_odd, right, left_near, left_far):
    size = vl.shape[0]
    height = size // 2
    even = lax.axis_index("space") % 2 == 0

    def fill(first, second):
        right[pl.ds(0, size)] = first
        right[pl.ds(size, size)] = second

    @pl.when(even)
    def _():
        fill(up_even[...], vl[...].T)

    @pl.when(jnp.logical_not(even))
    def _():
        fill(vl[...].T, up_odd[...])

    mine = order(0) // (lax.axis_size("energy") // 2)
    for pair in range(2):
        for j, left in enumerate((left_near, left_far)):
            at = pl.multiple_of(pair * size + (mine ^ j) * height, height)
            left[pair] = right[pl.ds(at, height)].T


def abreast(parts, wide):
    cols = parts.shape[2]
    for part in range(2):
        wide[:, part * cols : (part + 1) * cols] = parts[part]


def near_kernel(left, even, odd, out, wide):
    for pair, met in enumerate((even, odd)):
        abreast(met, wide)
        out[pair] = dot(left[pair], wide[...], NN)


def screen_kernel(order, right, left, begun, own, even, odd, *refs):
    outs, wide, product, total = refs[:-3], *refs[-3:]
    size, cols = total.shape[1:]
    for pair, met in enumerate((even, odd)):
        abreast(met, wide)
        both = (begun[pair] + dot(left[pair], wide[...], NN)).astype(BF16)
        for part in range(2):
            product[part * size : (part + 1) * size, pair * size : (pair + 1) * size] = both[:, part * cols : (part + 1) * cols]
    for part in range(2):
        total[part] = (own[part] + dot(product[part * size : (part + 1) * size], right[...], NN)).astype(BF16)
    rows = outs[0].shape[1]
    for j, out in enumerate(outs):
        at = pl.multiple_of(order(j) * rows, rows)
        for part in range(2):
            out[part] = total[part, pl.ds(at, rows)]


def call(kernel, outs, args, tables=0, scratch=(), flops=0):
    traffic = sum(x.size * x.dtype.itemsize for x in (*args, *outs))
    return pl.pallas_call(
        kernel,
        out_shape=outs,
        in_specs=[smem()] * tables + [vmem()] * (len(args) - tables),
        out_specs=[vmem()] * len(outs),
        scratch_shapes=scratch,
        compiler_params=pltpu.CompilerParams(vmem_limit_bytes=VMEM_LIMIT),
        cost_estimate=pl.CostEstimate(flops=flops, bytes_accessed=traffic, transcendentals=0),
    )(*args)


def struct(shape, kind=BF16):
    return jax.ShapeDtypeStruct(shape, kind)


def direct(energies, green, v_diag, v_low, energy_slot):
    parts = lax.axis_size("energy")
    layers = lax.axis_size("space")
    block, cols = green.shape[3:]
    rows = block // parts
    scaling = energies ** (-0.5)

    def order(j):
        return lax.axis_index("energy") ^ j

    def swap(pieces, sequence):
        out = list(pieces)
        for j in sequence:
            out[j] = lax.ppermute(pieces[j], "energy", [(i, i ^ j) for i in range(parts)])
        return out

    def meet(value):
        out = []
        for first in range(2):
            lows = range(first, layers - 1, 2)
            out.append(lax.ppermute(value, "space", [p for i in lows for p in ((i, i + 1), (i + 1, i))]))
        return out

    def take(partners):
        return pl.pallas_call(
            functools.partial(cut_kernel, order, partners),
            out_shape=[struct((green.shape[0], rows, cols))] * len(partners),
            in_specs=[pl.BlockSpec(memory_space=pltpu.HBM)],
            out_specs=[vmem()] * len(partners),
            scratch_shapes=[pltpu.SemaphoreType.DMA((len(partners),))],
            compiler_params=pltpu.CompilerParams(vmem_limit_bytes=VMEM_LIMIT),
        )(pltpu.with_memory_space_constraint(green, pltpu.HBM))

    first, later = sequence_far(parts)[:2], (*sequence_far(parts)[2:], 0)
    cut = dict(zip(first + later, (*take(first), *take(later))))
    cut = [cut[j] for j in range(parts)]
    arrived = swap(cut, range(1, parts))
    upper = meet(v_low[0])
    piece = struct((2, rows, cols))
    *polar_out, lesser = call(
        functools.partial(polar_kernel, order, scaling),
        [piece] * parts + [struct((2, energies, rows, cols), F32)],
        [energy_slot] + arrived,
        tables=1,
        scratch=[pltpu.VMEM((2, energies, rows, cols), F32), pltpu.VMEM((energies, 2, rows, cols), F32)],
    )
    polar_in = swap(polar_out, range(1, parts))
    half = parts // 2
    part = struct((2, block // 2, cols))
    whole = struct((2, block, cols))
    own_halves, halves = [], ([], [])
    for h in range(2):
        pieces = polar_in[h * half : (h + 1) * half]
        own_halves.append(call(functools.partial(gather_kernel, order), [part], pieces)[0])
        for pair, value in enumerate(meet(own_halves[h])):
            halves[pair].append(value)
    work = 4 * block * block * cols
    own = call(
        functools.partial(own_kernel, order),
        [struct(whole.shape, F32)],
        [v_diag[0], *own_halves],
        scratch=[pltpu.VMEM(whole.shape, BF16)],
        flops=2 * work,
    )[0]
    left = struct((2, block, block // 2))
    right, left_near, left_far = call(
        functools.partial(couple_kernel, order), [struct((2 * block, block)), left, left], [v_low[0], *upper]
    )
    wide = pltpu.VMEM((block // 2, 2 * cols), BF16)
    begun = call(
        near_kernel,
        [struct((2, block, 2 * cols), F32)],
        [left_near, halves[0][0], halves[1][0]],
        scratch=[wide],
        flops=work,
    )[0]
    screened_out = call(
        functools.partial(screen_kernel, order),
        [piece] * parts,
        [right, left_far, begun, own, halves[0][1], halves[1][1]],
        scratch=[wide, pltpu.VMEM((2 * block, 2 * block), BF16), pltpu.VMEM(whole.shape, BF16)],
        flops=3 * work,
    )
    screened_in = swap(screened_out, range(1, parts))
    weights = pltpu.VMEM((half, 2, rows, cols), F32)
    part = call(
        functools.partial(early_kernel, order),
        [struct((2, energies, rows, cols), F32)],
        [lesser, *screened_in[::2]],
        scratch=[weights],
    )[0]
    return pl.pallas_call(
        functools.partial(sigma_kernel, order, scaling),
        name="sigma",
        out_shape=struct((2, energies, 1, rows, cols)),
        in_specs=[smem()] + [vmem()] * (half + 2),
        out_specs=pl.BlockSpec(memory_space=pltpu.HBM),
        scratch_shapes=[
            weights,
            pltpu.VMEM((2, energies, rows, cols), F32),
            pltpu.VMEM((2, energies, rows, cols), BF16),
            pltpu.SemaphoreType.DMA((rows // TILE,)),
        ],
        compiler_params=pltpu.CompilerParams(vmem_limit_bytes=VMEM_LIMIT),
    )(energy_slot, lesser, part, *screened_in[1::2])


def shifted(value, axis, steps):
    count = lax.axis_size(axis)
    leading, last = (max(0, -steps), min(count, count - steps))
    return lax.ppermute(value, axis, [(source, source + steps) for source in range(leading, last)])


def apply_table(table, values):
    return jnp.dot(
        table, values, precision=lax.Precision.HIGHEST, preferred_element_type=jnp.float32
    )


def spectra(cos_table, sin_table, real_part, imag_part):
    out_real = apply_table(cos_table, real_part) + apply_table(sin_table, imag_part)
    out_imag = apply_table(cos_table, imag_part) - apply_table(sin_table, real_part)
    return (out_real, out_imag)


def to_slots(cos_table, sin_table, real_part, imag_part):
    factor = 1.0 / cos_table.shape[0]
    cos_back = cos_table.T
    sin_back = sin_table.T
    out_real = (apply_table(cos_back, real_part) - apply_table(sin_back, imag_part)) * factor
    out_imag = (apply_table(cos_back, imag_part) + apply_table(sin_back, real_part)) * factor
    return (out_real, out_imag)


def sandwich(matrix, polar):
    left = jnp.einsum("ij,cejk->ceik", matrix, polar, preferred_element_type=jnp.float32).astype(
        jnp.bfloat16
    )
    return jnp.einsum("ceij,kj->ceik", left, matrix, preferred_element_type=jnp.float32)


def sandwich_t(matrix, polar):
    left = jnp.einsum("ji,cejk->ceik", matrix, polar, preferred_element_type=jnp.float32).astype(
        jnp.bfloat16
    )
    return jnp.einsum("ceij,jk->ceik", left, matrix, preferred_element_type=jnp.float32)


def general(green, v_diag, v_low, energy_slot):
    energies = energy_slot.shape[0]
    period = 2 * energies
    frequency = jnp.arange(period, dtype=jnp.int32)
    phases = frequency[:, None] * energy_slot[None, :] % period
    angles = phases.astype(jnp.float32) * (2.0 * math.pi / period)
    cos_table = jnp.cos(angles)
    sin_table = jnp.sin(angles)
    scaling = energies ** (-0.5)
    arrived = lax.all_to_all(green[:, :, 0], "energy", split_axis=2, concat_axis=1, tiled=True)
    row_count = arrived.shape[2]
    col_count = arrived.shape[3]
    flattened = arrived.reshape((4, energies, row_count * col_count)).astype(jnp.float32)
    lesser_re, lesser_im = spectra(cos_table, sin_table, flattened[0], flattened[1])
    greater_re, greater_im = spectra(cos_table, sin_table, flattened[2], flattened[3])
    cross_re = lesser_re * greater_re + lesser_im * greater_im
    cross_im = lesser_im * greater_re - lesser_re * greater_im
    corr_re, corr_im = to_slots(cos_table, sin_table, cross_re, cross_im)
    polar_slot = (
        jnp.stack([corr_im * scaling, -corr_re * scaling])
        .reshape((2, energies, row_count, col_count))
        .astype(jnp.bfloat16)
    )
    polar = lax.all_to_all(polar_slot, "energy", split_axis=1, concat_axis=2, tiled=True)
    diagonal = v_diag[0]
    lower = v_low[0]
    own_term = sandwich(diagonal, polar)
    below = shifted(polar, "space", 1)
    handed = sandwich_t(lower, polar).astype(jnp.bfloat16)
    received = shifted(handed, "space", -1)
    total = own_term + sandwich(lower, below) + received.astype(jnp.float32)
    screened = total.astype(jnp.bfloat16)
    screened_rows = lax.all_to_all(screened, "energy", split_axis=2, concat_axis=1, tiled=True)
    weights = screened_rows.reshape((2, energies, row_count * col_count)).astype(jnp.float32)
    weight_re, weight_im = spectra(cos_table, sin_table, weights[0], weights[1])
    joint_re = lesser_re * weight_re - lesser_im * weight_im
    joint_im = lesser_re * weight_im + lesser_im * weight_re
    conv_re, conv_im = to_slots(cos_table, sin_table, joint_re, joint_im)
    sigma = (
        jnp.stack([-conv_im * scaling, conv_re * scaling])
        .reshape((2, energies, row_count, col_count))
        .astype(jnp.bfloat16)
    )
    return sigma[:, :, None]


def sequence_far(parts):
    chips = [j for j in (6, 4, 2) if j < parts] + list(range(8, parts, 2))
    return (*(j + core for j in chips for core in range(2)), 1)


def solution(mesh):
    in_specs = (
        P(None, "energy", "space", None, None),
        P("space", None, None),
        P("space", None, None),
        P(),
    )
    out_specs = P(None, None, "space", "energy", None)
    parts = mesh.shape["energy"]
    paired = parts & (parts - 1) == 0 and 4 <= parts <= PAIRED and mesh.shape["space"] > 2

    def whole(green, v_diag, v_low, energy_slot):
        rows = green.shape[3] // parts
        fast = paired and parts == energy_slot.shape[0] and rows % SUBLANES == 0
        body = functools.partial(direct, parts) if fast else general
        return jax.shard_map(body, mesh=mesh, in_specs=in_specs, out_specs=out_specs, check_vma=False)(
            green, v_diag, v_low, energy_slot
        )

    return whole
```
